256 devices in a mesh: grp: 4 (over y), seq: 64 (over z, x, core).
Axes of the slice: x: 4, y: 4, z: 8, core: 2. Of those that a mesh axis runs over, the one named last changes fastest.
Arguments:
- tokens: bfloat16 [1024, 1024], P(('grp', 'seq')), may hold values from -6 to 6
- attn_gain: float32 [1024], replicated, may hold values from 0.1 to 1.9
- w_qkv: bfloat16 [1024, 3072], replicated, may hold values from -0.1875 to 0.1875
- w_out: bfloat16 [1024, 1024], replicated, may hold values from -0.1875 to 0.1875
- mlp_gain: float32 [1024], replicated, may hold values from 0.1 to 1.9
- w_gate_up: bfloat16 [2, 1024, 4096], P(None, None, 'seq'), may hold values from -0.1875 to 0.1875
- w_down: bfloat16 [4096, 1024], P('seq'), may hold values from -0.09375 to 0.09375
- kv_cache: bfloat16 [3072, 2, 64, 1024], P(('grp', 'seq'))
- block_owner: int32 [3072], P(('grp', 'seq')), may hold values from 0 to 255, as said below
- block_fill: int32 [3072], P(('grp', 'seq')), may hold values from 0 to 64, as said below
Outputs:
- output: bfloat16 [1024, 1024], P(('grp', 'seq'))
The draws below stay inside these ranges and needn't reach their ends.
Inputs may be any that keep to these rules, and one draw needn't show every extreme that they name: `block_fill`: each request has at least one block; in each group one request fills exactly 256 whole blocks, every other has at most 2 blocks; blocks of one request are live from their start and all but its last are full; blocks with no live token exist in every group. `block_owner`: every served request number of a group names some block of that group.
All inputs are finite; a program needn't handle non-finite values.
Results may differ from the reference program's by a relative error of at most 0.024.
Values may be sent and summed in bfloat16 or wider, within the bound.
No kernel may reach another device: no remote copies, remote signals or barrier semaphores. Data moves between devices by JAX's collectives and lax.ppermute only.
A program may use at most 320 MiB of HBM per device.

```python
import jax
import jax.numpy as jnp
from jax import lax

D = 1024
HEADS = 16
HD = 64
FF = 4096
BLK = 64
REQ_DEV = 4
GROUPS = 4
SHARDS = 64
REQ_GRP = 256
REQUESTS = 1024
NBLOCKS = 768
LONG_BLOCKS = 256
SHORT_BLOCKS = 2


def block_layout(key):
    base_key = jax.random.fold_in(key, 7)

    def one_group(group_key):
        k_count, k_long, k_tail, k_order = jax.random.split(group_key, 4)
        requests = jnp.arange(REQ_GRP, dtype=jnp.int32)
        counts = jax.random.randint(k_count, (REQ_GRP,), 1, SHORT_BLOCKS + 1)
        longest = jax.random.randint(k_long, (), 0, REQ_GRP)
        counts = jnp.where(requests == longest, LONG_BLOCKS, counts).astype(jnp.int32)
        tail_fill = jax.random.randint(k_tail, (REQ_GRP,), 1, BLK + 1)
        tail_fill = jnp.where(requests == longest, BLK, tail_fill).astype(jnp.int32)
        end_slots = jnp.cumsum(counts).astype(jnp.int32)
        slot_ids = jnp.arange(NBLOCKS, dtype=jnp.int32)
        owners = jnp.minimum(jnp.searchsorted(end_slots, slot_ids, side='right'), REQ_GRP - 1).astype(jnp.int32)
        is_used = slot_ids < end_slots[REQ_GRP - 1]
        is_last = slot_ids == jnp.take(end_slots, owners) - 1
        filled = jnp.where(is_used, jnp.where(is_last, jnp.take(tail_fill, owners), BLK), 0).astype(jnp.int32)
        owners = jnp.where(is_used, owners, slot_ids % REQ_GRP).astype(jnp.int32)
        shuffle = jax.random.permutation(k_order, NBLOCKS)
        return (jnp.take(owners, shuffle), jnp.take(filled, shuffle))
    group_keys = jax.vmap(lambda group_index: jax.random.fold_in(base_key, group_index))(jnp.arange(GROUPS))
    owners, filled = jax.vmap(one_group)(group_keys)
    return (owners.reshape(-1).astype(jnp.int32), filled.reshape(-1).astype(jnp.int32))


def draw_block_owner(key, part):
    return block_layout(key)[0]


def draw_block_fill(key, part):
    return block_layout(key)[1]


def draw_kv_cache(key, part):
    full_shape = (GROUPS * NBLOCKS, 2, BLK, D)
    values = jnp.clip(jax.random.normal(key, full_shape, jnp.float32), -6.0, 6.0)
    return values.astype(jnp.bfloat16)


def steps_of(key, extent, cuts, least, largest):
    def one(dim, shards_of):
        heights = jax.random.uniform(jax.random.fold_in(jax.random.fold_in(key, 6), dim), (shards_of,), jnp.float32, least / len(cuts), largest / len(cuts))
        return jnp.repeat(jnp.exp(heights), extent[dim] // shards_of).reshape((-1,) + (1,) * (len(extent) - dim - 1))

    factor_of = one(*cuts[0])
    for cut in cuts[1:]:
        factor_of = factor_of * one(*cut)
    return factor_of


def centred(stream_key, dims, deviation, most, cuts=(), held_as=jnp.bfloat16):
    array = jax.random.normal(stream_key, dims, jnp.float32) * deviation
    if len(cuts) > 0:
        array = steps_of(stream_key, dims, cuts, -0.22, 0.18) * array
    return jnp.clip(array, min=-most, max=most).astype(held_as)


def setup_inputs(seed: int = 0) -> dict:
    key_of = jax.random.split(jax.random.key(seed), 11)
    tokens = centred(key_of[0], (REQUESTS, D), 1.0, 6.0, ((0, 256),))
    attn_gain = jnp.clip(1.0 + 0.18 * jax.random.normal(key_of[1], (D,), jnp.float32), 0.1, 1.9)
    w_qkv = centred(key_of[2], (D, 3 * D), D ** -0.5, 0.1875)
    w_out = centred(key_of[3], (D, D), D ** -0.5, 0.1875)
    mlp_gain = jnp.clip(1.0 + 0.18 * jax.random.normal(key_of[4], (D,), jnp.float32), 0.1, 1.9)
    w_gate_up = centred(key_of[5], (2, D, FF), D ** -0.5, 0.1875, ((2, 64),))
    w_down = centred(key_of[6], (FF, D), FF ** -0.5, 0.09375, ((0, 64),))
    kv_cache = draw_kv_cache(jax.random.fold_in(key_of[10], 71), 0)
    block_owner = draw_block_owner(jax.random.fold_in(key_of[10], 71), 0)
    block_fill = draw_block_fill(jax.random.fold_in(key_of[10], 71), 0)
    return dict(tokens=tokens, attn_gain=attn_gain, w_qkv=w_qkv, w_out=w_out, mlp_gain=mlp_gain, w_gate_up=w_gate_up, w_down=w_down, kv_cache=kv_cache, block_owner=block_owner, block_fill=block_fill)


floor_score = -1e+30
epsilon = 1e-05

def rms_scaled(row_data, gain):
    values = row_data.astype(jnp.float32)
    return values * lax.rsqrt(lax.optimization_barrier(jnp.mean(values * values, axis=-1, keepdims=True)) + epsilon) * gain

def served_rows(group_id):
    slot_ids = jnp.arange(REQ_GRP, dtype=jnp.int32)
    return (slot_ids % GROUPS * SHARDS + slot_ids // REQ_DEV) * REQ_DEV + slot_ids % REQ_DEV // GROUPS * GROUPS + group_id

def reference(tokens, attn_gain, w_qkv, w_out, mlp_gain, w_gate_up, w_down, kv_cache, block_owner, block_fill):
    normed = rms_scaled(tokens, attn_gain).astype(jnp.bfloat16)
    qkv = jnp.dot(normed, w_qkv, preferred_element_type=jnp.float32).astype(jnp.bfloat16)
    query = qkv[:, :D]
    key_new = qkv[:, D:2 * D]
    value_new = qkv[:, 2 * D:]
    served_order = jax.vmap(served_rows)(jnp.arange(GROUPS, dtype=jnp.int32))
    caches = kv_cache.reshape(GROUPS, NBLOCKS, 2, BLK, D)
    owners = block_owner.reshape(GROUPS, NBLOCKS).astype(jnp.int32)
    fills = block_fill.reshape(GROUPS, NBLOCKS).astype(jnp.int32)
    score_scale = HD ** (-0.5)

    def attend(inputs):
        row_index, group_cache, owner_ids, filled = inputs
        query_rows = query[row_index].astype(jnp.float32).reshape(REQ_GRP, HEADS, HD)
        key_rows = key_new[row_index].astype(jnp.float32).reshape(REQ_GRP, HEADS, HD)
        value_rows = value_new[row_index].astype(jnp.float32).reshape(REQ_GRP, HEADS, HD)
        key_block = group_cache[:, 0].astype(jnp.float32).reshape(NBLOCKS, BLK, HEADS, HD)
        value_block = group_cache[:, 1].astype(jnp.float32).reshape(NBLOCKS, BLK, HEADS, HD)
        scores = jnp.einsum('bhd,bthd->bht', query_rows[owner_ids], key_block) * score_scale
        is_valid = jnp.arange(BLK, dtype=jnp.int32)[None, None, :] < filled[:, None, None]
        masked = jnp.where(is_valid, scores, floor_score)
        block_max = lax.optimization_barrier(jnp.max(masked, axis=2))
        rounded = lax.optimization_barrier(jnp.where(is_valid, jnp.exp(masked - block_max[:, :, None]), 0.0).astype(jnp.bfloat16))
        weights = rounded.astype(jnp.float32)
        block_total = lax.optimization_barrier(jnp.sum(weights, axis=2))
        block_sum = jnp.einsum('bht,bthd->bhd', weights, value_block)
        own_score = lax.optimization_barrier(jnp.sum(query_rows * key_rows, axis=2)) * score_scale
        maxima = jnp.maximum(jax.ops.segment_max(block_max, owner_ids, num_segments=REQ_GRP), own_score)
        factor = jnp.exp(block_max - maxima[owner_ids])
        own_weight = jnp.exp(own_score - maxima)
        totals = jax.ops.segment_sum(block_total * factor, owner_ids, num_segments=REQ_GRP) + own_weight
        weighted = jax.ops.segment_sum(block_sum * factor[:, :, None], owner_ids, num_segments=REQ_GRP) + value_rows * own_weight[:, :, None]
        return (weighted / totals[:, :, None]).reshape(REQ_GRP, D).astype(jnp.bfloat16)
    contexts = lax.map(attend, (served_order, caches, owners, fills))
    context = jnp.zeros((REQUESTS, D), jnp.bfloat16).at[served_order.reshape(-1)].set(contexts.reshape(-1, D))
    mixed_rows = tokens.astype(jnp.float32) + jnp.dot(context, w_out, preferred_element_type=jnp.float32)
    normed_mlp = rms_scaled(mixed_rows, mlp_gain).astype(jnp.bfloat16)
    gate_part = jnp.dot(normed_mlp, w_gate_up[0], preferred_element_type=jnp.float32)
    up_part = jnp.dot(normed_mlp, w_gate_up[1], preferred_element_type=jnp.float32)
    hidden = (jax.nn.silu(gate_part) * up_part).astype(jnp.bfloat16)
    return (mixed_rows + jnp.dot(hidden, w_down, preferred_element_type=jnp.float32)).astype(jnp.bfloat16)
```

```python
import jax
import jax.numpy as jnp
from jax import lax
from jax.experimental import pallas as pl
from jax.experimental.pallas import tpu as pltpu
from jax.sharding import Mesh, PartitionSpec as P

HEADS = 16
CORES = 2
LANES = 128
FLOOR = -1e30
EPSILON = 1e-05
F32 = jnp.float32
BF16 = jnp.bfloat16


def iota(shape, dim):
    return lax.broadcasted_iota(jnp.int32, shape, dim)


def dot(a, b):
    return jnp.dot(a, b, preferred_element_type=F32)


def pieces(v):
    high = v.astype(BF16)
    return high, (v - high.astype(F32)).astype(BF16)


def head_rows(feature_count, head_dim):
    shape = (LANES, feature_count)
    return (iota(shape, 1) // head_dim == iota(shape, 0)).astype(BF16)


def attend_kernel(owner, fill, got, peer, gain, w_qkv, kv, rows_out, own_out, *, rows, chips, head_dim):
    blocks, _, span, features = kv.shape
    half = got.shape[0]
    count = blocks + rows
    core = lax.axis_index("core")
    chip = lax.axis_index("chip")
    shape = (count, 2 * half)
    line = iota(shape, 0)
    place = jnp.zeros(shape, jnp.int32)
    owner_line = iota((count, LANES), 0)
    owners = jnp.zeros((count, LANES), jnp.int32)
    for b in range(blocks):
        u = owner[b]
        s = u // rows
        at = jnp.where(s % CORES == core, 0, half) + (u % rows) * chips + s // CORES
        place = jnp.where(line == b, at, place)
        owners = jnp.where(owner_line == b, u, owners)
    for i in range(rows):
        place = jnp.where(line == blocks + i, i * chips + chip, place)
        owners = jnp.where(owner_line == blocks + i, (chip * CORES + core) * rows + i, owners)
    select = (place == iota(shape, 1)).astype(BF16)
    inputs = dot(select[:, :half], got[...]) + dot(select[:, half:], peer[...])
    own_out[...] = inputs
    scale = lax.rsqrt(jnp.mean(inputs * inputs, axis=1, keepdims=True) + EPSILON)
    normed = (inputs * scale * gain[...]).astype(BF16)
    qkv = dot(normed, w_qkv[...]).astype(BF16).astype(F32)
    query = qkv[:, :features]
    key_new = qkv[:, features : 2 * features]
    value_new = qkv[:, 2 * features :]

    head_mask = iota((HEADS, features), 1) // head_dim == iota((HEADS, features), 0)
    spread = jnp.concatenate(
        [
            jnp.where(head_mask, jnp.broadcast_to(query[b : b + 1], (HEADS, features)), 0.0)
            for b in range(blocks)
        ],
        axis=0,
    ).astype(BF16)
    keys = kv[:, 0].reshape(blocks * span, features)
    values = kv[:, 1].reshape(blocks * span, features)
    scores = lax.dot_general(
        spread, keys, (((1,), (1,)), ((), ())), preferred_element_type=F32
    ) * (head_dim**-0.5)
    wide = scores.shape
    column = iota(wide, 1)
    column_block = column // span
    limit = jnp.zeros((1, blocks * span), jnp.int32)
    limit_block = iota(limit.shape, 1) // span
    for b in range(blocks):
        limit = jnp.where(limit_block == b, fill[b], limit)
    live = (column_block == iota(wide, 0) // HEADS) & (column - column_block * span < limit)
    masked = jnp.where(live, scores, FLOOR)
    peak = jnp.max(masked, axis=1, keepdims=True)
    weights = jnp.where(live, jnp.exp(masked - peak), 0.0).astype(BF16)
    total = jnp.sum(weights.astype(F32), axis=1, keepdims=True)
    summed = dot(weights, values)
    alive = total > 0.0
    safe = jnp.where(alive, total, 1.0)
    level = jnp.where(alive, peak + jnp.log(safe), FLOOR)
    summed = summed * (1.0 / safe)
    diagonal = iota((HEADS, LANES), 0) == iota((HEADS, LANES), 1)
    for b in range(blocks):
        part = slice(b * HEADS, (b + 1) * HEADS)
        rows_out[b : b + 1, :features] = jnp.sum(
            jnp.where(head_mask, summed[part], 0.0), axis=0, keepdims=True
        )
        rows_out[b : b + 1, features : features + LANES] = jnp.sum(
            jnp.where(diagonal, level[part], 0.0), axis=0, keepdims=True
        )
    shape = (features, LANES)
    by_head = (iota(shape, 0) // head_dim == iota(shape, 1)).astype(BF16)
    high, low = pieces(query * key_new)
    own_score = (dot(high, by_head) + dot(low, by_head)) * (head_dim**-0.5)
    rows_out[blocks:, :features] = value_new[blocks:]
    rows_out[blocks:, features : features + LANES] = own_score[blocks:]
    rows_out[:, features + LANES :] = owners.astype(F32)


def merge_kernel(mine, peer, out, *, rows, head_dim):
    count = 2 * mine.shape[0]
    features = mine.shape[1] - 2 * LANES
    half = out.shape[0]
    core = lax.axis_index("core")
    values = jnp.concatenate([mine[:, :features], peer[:, :features]], axis=0)
    level = jnp.concatenate(
        [mine[:, features : features + LANES], peer[:, features : features + LANES]], axis=0
    )
    owners = jnp.concatenate([mine[:, features + LANES :], peer[:, features + LANES :]], axis=0)
    square = (count, count)
    owner_column = owners[:, :1]
    owner_row = jnp.sum(
        jnp.where(iota(square, 0) == iota(square, 1), owner_column, 0.0), axis=0, keepdims=True
    )
    same = owner_column == owner_row
    peak = jnp.full(level.shape, FLOOR, F32)
    for j in range(count):
        peak = jnp.maximum(
            peak, jnp.where(owners == owners[j : j + 1], level[j : j + 1], FLOOR)
        )
    weight = jnp.exp(level - peak)
    same_table = same.astype(BF16)
    high, low = pieces(weight)
    total = dot(same_table, high) + dot(same_table, low)
    joined = jnp.where(iota(level.shape, 1) < HEADS, peak + jnp.log(total), 0.0)
    heads = head_rows(features, head_dim)
    high, low = pieces(weight / total)
    scaled = values * (dot(high, heads) + dot(low, heads))
    first = (
        jnp.sum(
            jnp.where(same & (iota(square, 0) < iota(square, 1)), 1.0, 0.0), axis=0, keepdims=True
        )
        == 0.0
    )
    owner_row = owner_row.astype(jnp.int32)
    home = owner_row // rows
    place = jnp.where(home % CORES == core, (home // CORES) * rows + owner_row % rows, -1)
    chosen = iota((half, count), 0) == place
    table = chosen.astype(BF16)
    high, low = pieces(scaled)
    out[:, :features] = (dot(table, high) + dot(table, low)).astype(BF16)
    one = joined.astype(BF16)
    rest = joined - one.astype(F32)
    two = rest.astype(BF16)
    three = (rest - two.astype(F32)).astype(BF16)
    packed = (
        one.astype(F32)
        + pltpu.roll(two.astype(F32), HEADS, 1)
        + pltpu.roll(three.astype(F32), 2 * HEADS, 1)
    ).astype(BF16)
    first_table = (chosen & first).astype(BF16)
    stats = dot(first_table, packed)
    absent = jnp.sum(table.astype(F32), axis=1, keepdims=True) == 0.0
    out[:, features:] = jnp.where(
        absent & (iota(stats.shape, 1) < HEADS), FLOOR, stats
    ).astype(BF16)


def project_kernel(got, inputs, w_out, gain, mixed_out, sent, *, rows, head_dim):
    half = got.shape[0]
    features = w_out.shape[0]
    sub = 8
    parts = half // sub
    stats = got[:, features:].astype(F32)
    level = stats + pltpu.roll(stats, LANES - HEADS, 1) + pltpu.roll(stats, LANES - 2 * HEADS, 1)
    level = jnp.where(iota(level.shape, 1) < HEADS, level, FLOOR)
    level = level.reshape(parts, sub, LANES)
    peak = jnp.max(level, axis=0)
    peak = jnp.maximum(peak, pltpu.roll(peak, rows, 0))
    weight = jnp.exp(level - peak[None])
    total = jnp.sum(weight, axis=0)
    total = total + pltpu.roll(total, rows, 0)
    weight = (weight / total[None]).reshape(half, LANES)
    heads = head_rows(features, head_dim)
    high, low = pieces(weight)
    spread = dot(high, heads) + dot(low, heads)
    scaled = got[:, :features].astype(F32) * spread
    weighted = jnp.sum(scaled.reshape(parts, sub, features), axis=0)
    context = (weighted + pltpu.roll(weighted, rows, 0)).astype(BF16)
    last = inputs[inputs.shape[0] - sub :, :]
    last = jnp.where(iota(last.shape, 0) < rows, pltpu.roll(last, rows, 0), last)
    mixed = last + dot(context, w_out[...])
    mixed_out[...] = mixed
    scale = lax.rsqrt(jnp.mean(mixed * mixed, axis=1, keepdims=True) + EPSILON)
    normed = mixed * scale * gain[...]
    sent[...] = jnp.concatenate([normed] * parts, axis=0).astype(BF16)


def hidden_kernel(got, peer, w_gate_up, w_down, mixed, own_out, sent, *, rows, chips):
    half = got.shape[0]
    chip = lax.axis_index("chip")
    shape = (half, half)
    line = iota(shape, 0)
    order = (iota(shape, 1) == (line % chips) * rows + line // chips).astype(BF16)

    def down(part):
        gate = dot(part, w_gate_up[0])
        up = dot(part, w_gate_up[1])
        hidden = (gate / (1.0 + jnp.exp(-gate)) * up).astype(BF16)
        return dot(dot(order, hidden).astype(BF16), w_down[...])

    sent[...] = down(peer[...]).astype(BF16)
    own_out[...] = down(got[...])
    for i in range(rows):
        at = pl.ds(i * chips + chip, 1)
        own_out[at, :] = own_out[at, :] + mixed[i : i + 1, :]


def call(kernel, out_shape, smem=0, args=(), limit=48 << 20):
    vmem = pl.BlockSpec(memory_space=pltpu.VMEM)
    scalar = pl.BlockSpec(memory_space=pltpu.SMEM)
    specs = [scalar] * smem + [vmem] * (len(args) - smem)
    return pl.pallas_call(
        kernel,
        out_shape=out_shape,
        in_specs=specs,
        out_specs=jax.tree.map(lambda _: vmem, out_shape),
        compiler_params=pltpu.CompilerParams(vmem_limit_bytes=limit),
    )(*args)


def body(
    tokens, attn_gain, w_qkv, w_out, mlp_gain, w_gate_up, w_down, kv_cache, block_owner, block_fill
):
    groups = lax.axis_size("grp")
    chips = lax.axis_size("chip")
    rows, features = tokens.shape
    head_dim = features // HEADS
    blocks = kv_cache.shape[0]
    half = rows * chips
    count = blocks + rows
    swap = [(0, 1), (1, 0)]
    every = ("grp", "chip")

    def shape(dims, kind):
        return jax.ShapeDtypeStruct(dims, kind)

    sent = jnp.broadcast_to(tokens[:, None, :], (groups, chips, features))
    got = lax.all_to_all(sent.reshape(groups * chips, features), every, 0, 0, tiled=True)
    peer = lax.ppermute(got, "core", swap)
    partial, inputs = call(
        lambda *refs: attend_kernel(*refs, rows=rows, chips=chips, head_dim=head_dim),
        (shape((count, features + 2 * LANES), F32), shape((count, features), F32)),
        smem=2,
        args=(block_owner, block_fill, got, peer, attn_gain.reshape(1, features), w_qkv, kv_cache),
    )
    partial_peer = lax.ppermute(partial, "core", swap)
    sent = call(
        lambda *refs: merge_kernel(*refs, rows=rows, head_dim=head_dim),
        shape((half, features + LANES), BF16),
        args=(partial, partial_peer),
    )
    got = lax.all_to_all(sent, "chip", 0, 0, tiled=True)
    mixed, sent = call(
        lambda *refs: project_kernel(*refs, rows=rows, head_dim=head_dim),
        (shape((8, features), F32), shape((half, features), BF16)),
        args=(got, inputs, w_out, mlp_gain.reshape(1, features)),
    )
    got = lax.all_to_all(sent, "chip", 0, 0, tiled=True)
    peer = lax.ppermute(got, "core", swap)
    own, sent = call(
        lambda *refs: hidden_kernel(*refs, rows=rows, chips=chips),
        (shape((half, features), F32), shape((half, features), BF16)),
        args=(got, peer, w_gate_up, w_down, mixed),
    )
    peer = lax.ppermute(sent, "core", swap)
    sent = (own + peer.astype(F32)).astype(BF16)
    got = lax.all_to_all(sent, every, 0, 0, tiled=True)
    output = jnp.sum(got.reshape(groups, chips, features).astype(F32), axis=1)
    return output.astype(BF16)


def solution(mesh):
    groups, shards = mesh.devices.shape
    devices = mesh.devices.reshape(groups, shards // CORES, CORES)
    fine = Mesh(devices, ("grp", "chip", "core"))
    seq = ("chip", "core")
    whole = ("grp", "chip", "core")
    in_specs = (
        P(whole, None),
        P(),
        P(),
        P(),
        P(),
        P(None, None, seq),
        P(seq, None),
        P(whole, None, None, None),
        P(whole),
        P(whole),
    )
    return jax.shard_map(
        body, mesh=fine, in_specs=in_specs, out_specs=P(whole, None), check_vma=False
    )
```

```python
import jax
import jax.numpy as jnp
from jax import lax
from jax.experimental import pallas as pl
from jax.experimental.pallas import tpu as pltpu
from jax.sharding import Mesh, PartitionSpec as P

HEADS = 16
CORES = 2
LANES = 128
SUB = 8
FLOOR = -1e30
EPSILON = 1e-05
F32 = jnp.float32
BF16 = jnp.bfloat16


def iota(shape, dim):
    return lax.broadcasted_iota(jnp.int32, shape, dim)


def dot(a, b):
    return jnp.dot(a, b, preferred_element_type=F32)


def pieces(v):
    high = v.astype(BF16)
    return high, (v - high.astype(F32)).astype(BF16)


def head_rows(feature_count, head_dim):
    shape = (LANES, feature_count)
    return (iota(shape, 1) // head_dim == iota(shape, 0)).astype(BF16)


def lay_flat(tiles):
    return jnp.concatenate([tiles[:, j, :] for j in range(SUB)], axis=1)


def spread_kernel(tokens, out, tiles, *, chips):
    rows, features = tokens.shape
    width = features // SUB
    values = tokens[...].astype(F32)
    for j in range(SUB):
        tiles[:, j, :] = values[:, j * width : (j + 1) * width]
    for g in range(rows):
        row = tiles[g].astype(BF16)
        out[g * chips : (g + 1) * chips] = jnp.broadcast_to(row[None], (chips,) + row.shape)


def finish_kernel(got, out, tiles, *, chips):
    rows, features = out.shape
    width = features // SUB
    for g in range(rows):
        tiles[g] = jnp.sum(got[g * chips : (g + 1) * chips].astype(F32), axis=0)
    out[...] = lay_flat(tiles).astype(BF16)


def rms_scaled(values, gain):
    scale = lax.rsqrt(jnp.mean(values * values, axis=1, keepdims=True) + EPSILON)
    return (values * scale * gain).astype(BF16)


def own_kernel(got, gain, w_qkv, rows_out, own_out, tiles, *, rows, chips, head_dim):
    core = lax.axis_index("core")
    chip = lax.axis_index("chip")
    for k in range(SUB):
        tiles[k] = got[(k % rows) * chips + chip].astype(F32)
    inputs = lay_flat(tiles)
    own_out[...] = inputs
    features = inputs.shape[1]
    qkv = dot(rms_scaled(inputs, gain[...]), w_qkv[...]).astype(BF16).astype(F32)
    query = qkv[:, :features]
    key_new = qkv[:, features : 2 * features]
    shape = (features, LANES)
    by_head = (iota(shape, 0) // head_dim == iota(shape, 1)).astype(BF16)
    high, low = pieces(query * key_new)
    rows_out[:, :features] = qkv[:, 2 * features :]
    rows_out[:, features : features + LANES] = (dot(high, by_head) + dot(low, by_head)) * (
        head_dim**-0.5
    )
    owners = (chip * CORES + core) * rows + iota((SUB, LANES), 0) % rows
    rows_out[:, features + LANES :] = owners.astype(F32)


def attend_kernel(
    owner, fill, got, peer, own, gain, w_qkv, kv, rows_out, tiles, *, rows, chips, head_dim
):
    blocks, _, span, features = kv.shape
    core = lax.axis_index("core")
    owner_line = iota((blocks, LANES), 0)
    owners = jnp.zeros((blocks, LANES), jnp.int32)
    for b in range(blocks):
        u = owner[b]
        s = u // rows
        at = (u % rows) * chips + s // CORES
        tiles[b] = jnp.where(s % CORES == core, got[at].astype(F32), peer[at].astype(F32))
        owners = jnp.where(owner_line == b, u, owners)
    inputs = lay_flat(tiles)
    query = dot(rms_scaled(inputs, gain[...]), w_qkv[:, :features]).astype(BF16).astype(F32)

    head_mask = iota((HEADS, features), 1) // head_dim == iota((HEADS, features), 0)
    spread = jnp.concatenate(
        [
            jnp.where(head_mask, jnp.broadcast_to(query[b : b + 1], (HEADS, features)), 0.0)
            for b in range(blocks)
        ],
        axis=0,
    ).astype(BF16)
    keys = kv[:, 0].reshape(blocks * span, features)
    values = kv[:, 1].reshape(blocks * span, features)
    scores = lax.dot_general(
        spread, keys, (((1,), (1,)), ((), ())), preferred_element_type=F32
    ) * (head_dim**-0.5)
    wide = scores.shape
    column = iota(wide, 1)
    column_block = column // span
    limit = jnp.zeros((1, blocks * span), jnp.int32)
    limit_block = iota(limit.shape, 1) // span
    for b in range(blocks):
        limit = jnp.where(limit_block == b, fill[b], limit)
    live = (column_block == iota(wide, 0) // HEADS) & (column - column_block * span < limit)
    masked = jnp.where(live, scores, FLOOR)
    peak = jnp.max(masked, axis=1, keepdims=True)
    weights = jnp.where(live, jnp.exp(masked - peak), 0.0).astype(BF16)
    total = jnp.sum(weights.astype(F32), axis=1, keepdims=True)
    summed = dot(weights, values)
    alive = total > 0.0
    safe = jnp.where(alive, total, 1.0)
    level = jnp.where(alive, peak + jnp.log(safe), FLOOR)
    summed = summed * (1.0 / safe)
    diagonal = iota((HEADS, LANES), 0) == iota((HEADS, LANES), 1)
    for b in range(blocks):
        part = slice(b * HEADS, (b + 1) * HEADS)
        rows_out[b : b + 1, :features] = jnp.sum(
            jnp.where(head_mask, summed[part], 0.0), axis=0, keepdims=True
        )
        rows_out[b : b + 1, features : features + LANES] = jnp.sum(
            jnp.where(diagonal, level[part], 0.0), axis=0, keepdims=True
        )
    rows_out[:blocks, features + LANES :] = owners.astype(F32)
    rows_out[blocks:, :] = own[SUB - rows :, :]


def merge_kernel(mine, peer, out, *, rows, head_dim):
    count = 2 * mine.shape[0]
    features = mine.shape[1] - 2 * LANES
    half = out.shape[0]
    core = lax.axis_index("core")
    values = jnp.concatenate([mine[:, :features], peer[:, :features]], axis=0)
    level = jnp.concatenate(
        [mine[:, features : features + LANES], peer[:, features : features + LANES]], axis=0
    )
    owners = jnp.concatenate([mine[:, features + LANES :], peer[:, features + LANES :]], axis=0)
    square = (count, count)
    owner_column = owners[:, :1]
    owner_row = jnp.sum(
        jnp.where(iota(square, 0) == iota(square, 1), owner_column, 0.0), axis=0, keepdims=True
    )
    same = owner_column == owner_row
    peak = jnp.full(level.shape, FLOOR, F32)
    for j in range(count):
        peak = jnp.maximum(
            peak, jnp.where(owners == owners[j : j + 1], level[j : j + 1], FLOOR)
        )
    weight = jnp.exp(level - peak)
    same_table = same.astype(BF16)
    high, low = pieces(weight)
    total = dot(same_table, high) + dot(same_table, low)
    joined = jnp.where(iota(level.shape, 1) < HEADS, peak + jnp.log(total), 0.0)
    heads = head_rows(features, head_dim)
    high, low = pieces(weight / total)
    scaled = values * (dot(high, heads) + dot(low, heads))
    first = (
        jnp.sum(
            jnp.where(same & (iota(square, 0) < iota(square, 1)), 1.0, 0.0), axis=0, keepdims=True
        )
        == 0.0
    )
    owner_row = owner_row.astype(jnp.int32)
    home = owner_row // rows
    place = jnp.where(home % CORES == core, (home // CORES) * rows + owner_row % rows, -1)
    chosen = iota((half, count), 0) == place
    table = chosen.astype(BF16)
    high, low = pieces(scaled)
    out[:, :features] = (dot(table, high) + dot(table, low)).astype(BF16)
    one = joined.astype(BF16)
    rest = joined - one.astype(F32)
    two = rest.astype(BF16)
    three = (rest - two.astype(F32)).astype(BF16)
    packed = (
        one.astype(F32)
        + pltpu.roll(two.astype(F32), HEADS, 1)
        + pltpu.roll(three.astype(F32), 2 * HEADS, 1)
    ).astype(BF16)
    first_table = (chosen & first).astype(BF16)
    stats = dot(first_table, packed)
    absent = jnp.sum(table.astype(F32), axis=1, keepdims=True) == 0.0
    out[:, features:] = jnp.where(
        absent & (iota(stats.shape, 1) < HEADS), FLOOR, stats
    ).astype(BF16)


def project_kernel(got, inputs, w_out, gain, mixed_out, sent, *, rows, head_dim):
    half = got.shape[0]
    features = w_out.shape[0]
    sub = SUB
    parts = half // sub
    stats = got[:, features:].astype(F32)
    level = stats + pltpu.roll(stats, LANES - HEADS, 1) + pltpu.roll(stats, LANES - 2 * HEADS, 1)
    level = jnp.where(iota(level.shape, 1) < HEADS, level, FLOOR)
    level = level.reshape(parts, sub, LANES)
    peak = jnp.max(level, axis=0)
    peak = jnp.maximum(peak, pltpu.roll(peak, rows, 0))
    weight = jnp.exp(level - peak[None])
    total = jnp.sum(weight, axis=0)
    total = total + pltpu.roll(total, rows, 0)
    weight = (weight / total[None]).reshape(half, LANES)
    heads = head_rows(features, head_dim)
    high, low = pieces(weight)
    spread = dot(high, heads) + dot(low, heads)
    scaled = got[:, :features].astype(F32) * spread
    weighted = jnp.sum(scaled.reshape(parts, sub, features), axis=0)
    context = (weighted + pltpu.roll(weighted, rows, 0)).astype(BF16)
    mixed = inputs[...] + dot(context, w_out[...])
    width = features // SUB
    for j in range(SUB):
        mixed_out[:, j, :] = mixed[:, j * width : (j + 1) * width]
    sent[...] = jnp.concatenate([rms_scaled(mixed, gain[...]).astype(F32)] * parts, axis=0).astype(BF16)


def down_tiles(part, w_gate_up, w_down, tiles, *, rows, chips):
    half = part.shape[0]
    nt = (((1,), (1,)), ((), ()))
    gate = lax.dot_general(part[...], w_gate_up[0], nt, preferred_element_type=F32)
    up = lax.dot_general(part[...], w_gate_up[1], nt, preferred_element_type=F32)
    hidden = (gate / (1.0 + jnp.exp(-gate)) * up).astype(BF16)
    line = iota((half, half), 0)
    order = (iota((half, half), 1) == (line % chips) * rows + line // chips).astype(BF16)
    result = dot(dot(order, hidden).astype(BF16), w_down[...])
    width = result.shape[1] // SUB
    for j in range(SUB):
        tiles[:, j, :] = result[:, j * width : (j + 1) * width]


def peer_hidden_kernel(part, w_gate_up, w_down, out, tiles, *, rows, chips):
    down_tiles(part, w_gate_up, w_down, tiles, rows=rows, chips=chips)
    out[...] = tiles[...].astype(BF16)


def own_hidden_kernel(part, w_gate_up, w_down, mixed, out, *, rows, chips):
    down_tiles(part, w_gate_up, w_down, out, rows=rows, chips=chips)
    chip = lax.axis_index("chip")
    for i in range(rows):
        at = i * chips + chip
        out[at] = out[at] + mixed[i]


def call(kernel, out_shape, args, smem=0, scratch=(), limit=24 << 20, cost=None):
    vmem = pl.BlockSpec(memory_space=pltpu.VMEM)
    scalar = pl.BlockSpec(memory_space=pltpu.SMEM)
    specs = [scalar] * smem + [vmem] * (len(args) - smem)
    return pl.pallas_call(
        kernel,
        out_shape=out_shape,
        in_specs=specs,
        out_specs=jax.tree.map(lambda _: vmem, out_shape),
        scratch_shapes=[pltpu.VMEM(dims, F32) for dims in scratch],
        compiler_params=pltpu.CompilerParams(vmem_limit_bytes=limit),
        cost_estimate=cost,
    )(*args)


def body(
    tokens, attn_gain, w_qkv, w_out, mlp_gain, w_gate_up, w_down, kv_cache, block_owner, block_fill
):
    groups = lax.axis_size("grp")
    chips = lax.axis_size("chip")
    rows, features = tokens.shape
    head_dim = features // HEADS
    blocks = kv_cache.shape[0]
    half = rows * chips
    count = blocks + rows
    width = features // SUB
    swap = [(0, 1), (1, 0)]
    every = ("grp", "chip")
    sizes = dict(rows=rows, chips=chips)

    def shape(kind, *dims):
        return jax.ShapeDtypeStruct(dims, kind)

    sent = call(
        lambda *refs: spread_kernel(*refs, chips=chips),
        shape(BF16, groups * chips, SUB, width),
        (tokens,),
        scratch=[(rows, SUB, width)],
        cost=pl.CostEstimate(flops=10**11, transcendentals=0, bytes_accessed=1 << 18),
    )
    got = lax.all_to_all(sent, every, 0, 0, tiled=True)
    peer = lax.ppermute(got, "core", swap)
    gain = attn_gain.reshape(1, features)
    own, inputs = call(
        lambda *refs: own_kernel(*refs, head_dim=head_dim, **sizes),
        (shape(F32, SUB, features + 2 * LANES), shape(F32, SUB, features)),
        (got, gain, w_qkv),
        scratch=[(SUB, SUB, width)],
        cost=pl.CostEstimate(flops=1, transcendentals=0, bytes_accessed=1),
    )
    partial = call(
        lambda *refs: attend_kernel(*refs, head_dim=head_dim, **sizes),
        shape(F32, count, features + 2 * LANES),
        (block_owner, block_fill, got, peer, own, gain, w_qkv, kv_cache),
        smem=2,
        scratch=[(blocks, SUB, width)],
    )
    partial_peer = lax.ppermute(partial, "core", swap)
    sent = call(
        lambda *refs: merge_kernel(*refs, rows=rows, head_dim=head_dim),
        shape(BF16, half, features + LANES),
        (partial, partial_peer),
    )
    got = lax.all_to_all(sent, "chip", 0, 0, tiled=True)
    mixed, sent = call(
        lambda *refs: project_kernel(*refs, rows=rows, head_dim=head_dim),
        (shape(F32, SUB, SUB, width), shape(BF16, half, features)),
        (got, inputs, w_out, mlp_gain.reshape(1, features)),
    )
    got = lax.all_to_all(sent, "chip", 0, 0, tiled=True)
    peer = lax.ppermute(got, "core", swap)
    w_wide = jnp.swapaxes(w_gate_up, 1, 2)
    sent = call(
        lambda *refs: peer_hidden_kernel(*refs, **sizes),
        shape(BF16, half, SUB, width),
        (peer, w_wide, w_down),
        scratch=[(half, SUB, width)],
    )
    peer = lax.ppermute(sent, "core", swap)
    own = call(
        lambda *refs: own_hidden_kernel(*refs, **sizes),
        shape(F32, half, SUB, width),
        (got, w_wide, w_down, mixed),
    )
    sent = (own + peer.astype(F32)).astype(BF16)
    got = lax.all_to_all(sent, every, 0, 0, tiled=True)
    return call(
        lambda *refs: finish_kernel(*refs, chips=chips),
        shape(BF16, rows, features),
        (got,),
        scratch=[(rows, SUB, width)],
    )


def solution(mesh):
    groups, shards = mesh.devices.shape
    devices = mesh.devices.reshape(groups, shards // CORES, CORES)
    fine = Mesh(devices, ("grp", "chip", "core"))
    seq = ("chip", "core")
    whole = ("grp", "chip", "core")
    in_specs = (
        P(whole, None),
        P(),
        P(),
        P(),
        P(),
        P(None, None, seq),
        P(seq, None),
        P(whole, None, None, None),
        P(whole),
        P(whole),
    )
    return jax.shard_map(
        body, mesh=fine, in_specs=in_specs, out_specs=P(whole, None), check_vma=False
    )
```

```python
import jax
import jax.numpy as jnp
from jax import lax
from jax.experimental import pallas as pl
from jax.experimental.pallas import tpu as pltpu
from jax.sharding import Mesh, PartitionSpec as P

HEADS = 16
CORES = 2
X_CHIPS = 4
LANES = 128
SUB = 8
FLOOR = -1e30
EPSILON = 1e-05
CHIP = ("z", "x")
F32 = jnp.float32
BF16 = jnp.bfloat16


def iota(shape, dim):
    return lax.broadcasted_iota(jnp.int32, shape, dim)


def dot(a, b):
    return jnp.dot(a, b, preferred_element_type=F32)


def pieces(v):
    high = v.astype(BF16)
    return high, (v - high.astype(F32)).astype(BF16)


def head_rows(feature_count, head_dim):
    shape = (LANES, feature_count)
    return (iota(shape, 1) // head_dim == iota(shape, 0)).astype(BF16)


def lay_flat(tiles):
    return jnp.concatenate([tiles[:, j, :] for j in range(SUB)], axis=1)


def spread_kernel(tokens, w_gate_up, w_down, out, packed, held, tiles, sems, *, chips):
    rows, features = tokens.shape
    width = features // SUB
    units = w_down.shape[0]
    copies = [
        pltpu.make_async_copy(w_gate_up.at[0], packed.at[pl.ds(0, units)], sems.at[0]),
        pltpu.make_async_copy(w_gate_up.at[1], packed.at[pl.ds(units, units)], sems.at[1]),
        pltpu.make_async_copy(w_down, packed.at[pl.ds(2 * units, units)], sems.at[2]),
    ]
    first = pltpu.make_async_copy(tokens, held, sems.at[3])
    first.start()
    for copy in copies:
        copy.start()
    first.wait()
    values = held[...].astype(F32)
    for j in range(SUB):
        tiles[:, j, :] = values[:, j * width : (j + 1) * width]
    for g in range(rows):
        row = tiles[g].astype(BF16)
        out[g * chips : (g + 1) * chips] = jnp.broadcast_to(row[None], (chips,) + row.shape)
    for copy in copies:
        copy.wait()


def finish_kernel(got, out, tiles):
    rows = out.shape[0]
    sources = got.shape[0] // rows
    for g in range(rows):
        tiles[g] = jnp.sum(got[g * sources : (g + 1) * sources].astype(F32), axis=0)
    out[...] = lay_flat(tiles).astype(BF16)


def rms_scaled(values, gain):
    scale = lax.rsqrt(jnp.mean(values * values, axis=1, keepdims=True) + EPSILON)
    return (values * scale * gain).astype(BF16)


def own_kernel(got, gain, w_qkv, rows_out, own_out, tiles, *, rows, chips, head_dim):
    core = lax.axis_index("core")
    chip = lax.axis_index(CHIP)
    for k in range(SUB):
        tiles[k] = got[(k % rows) * chips + chip].astype(F32)
    inputs = lay_flat(tiles)
    own_out[...] = inputs
    features = inputs.shape[1]
    qkv = dot(rms_scaled(inputs, gain[...]), w_qkv[...]).astype(BF16).astype(F32)
    query = qkv[:, :features]
    key_new = qkv[:, features : 2 * features]
    shape = (features, LANES)
    by_head = (iota(shape, 0) // head_dim == iota(shape, 1)).astype(BF16)
    high, low = pieces(query * key_new)
    rows_out[:, :features] = qkv[:, 2 * features :]
    rows_out[:, features : features + LANES] = (dot(high, by_head) + dot(low, by_head)) * (
        head_dim**-0.5
    )
    owners = (chip * CORES + core) * rows + iota((SUB, LANES), 0) % rows
    rows_out[:, features + LANES :] = owners.astype(F32)


def attend_kernel(
    owner, fill, got, peer, own, gain, w_qkv, kv, rows_out, tiles, *, rows, chips, head_dim
):
    blocks, _, span, features = kv.shape
    core = lax.axis_index("core")
    owner_line = iota((blocks, LANES), 0)
    owners = jnp.zeros((blocks, LANES), jnp.int32)
    for b in range(blocks):
        u = owner[b]
        s = u // rows
        at = (u % rows) * chips + s // CORES
        tiles[b] = jnp.where(s % CORES == core, got[at].astype(F32), peer[at].astype(F32))
        owners = jnp.where(owner_line == b, u, owners)
    inputs = lay_flat(tiles)
    query = dot(rms_scaled(inputs, gain[...]), w_qkv[:, :features]).astype(BF16).astype(F32)

    head_mask = iota((HEADS, features), 1) // head_dim == iota((HEADS, features), 0)
    spread = jnp.concatenate(
        [
            jnp.where(head_mask, jnp.broadcast_to(query[b : b + 1], (HEADS, features)), 0.0)
            for b in range(blocks)
        ],
        axis=0,
    ).astype(BF16)
    keys = kv[:, 0].reshape(blocks * span, features)
    values = kv[:, 1].reshape(blocks * span, features)
    scores = lax.dot_general(
        spread, keys, (((1,), (1,)), ((), ())), preferred_element_type=F32
    ) * (head_dim**-0.5)
    wide = scores.shape
    column = iota(wide, 1)
    column_block = column // span
    limit = jnp.zeros((1, blocks * span), jnp.int32)
    limit_block = iota(limit.shape, 1) // span
    for b in range(blocks):
        limit = jnp.where(limit_block == b, fill[b], limit)
    live = (column_block == iota(wide, 0) // HEADS) & (column - column_block * span < limit)
    masked = jnp.where(live, scores, FLOOR)
    peak = jnp.max(masked, axis=1, keepdims=True)
    weights = jnp.where(live, jnp.exp(masked - peak), 0.0).astype(BF16)
    total = jnp.sum(weights.astype(F32), axis=1, keepdims=True)
    summed = dot(weights, values)
    alive = total > 0.0
    safe = jnp.where(alive, total, 1.0)
    level = jnp.where(alive, peak + jnp.log(safe), FLOOR)
    summed = summed * (1.0 / safe)
    diagonal = iota((HEADS, LANES), 0) == iota((HEADS, LANES), 1)
    for b in range(blocks):
        part = slice(b * HEADS, (b + 1) * HEADS)
        rows_out[b : b + 1, :features] = jnp.sum(
            jnp.where(head_mask, summed[part], 0.0), axis=0, keepdims=True
        )
        rows_out[b : b + 1, features : features + LANES] = jnp.sum(
            jnp.where(diagonal, level[part], 0.0), axis=0, keepdims=True
        )
    rows_out[:blocks, features + LANES :] = owners.astype(F32)
    rows_out[blocks:, :] = own[SUB - rows :, :]


def merge_kernel(mine, peer, out, flat, *, rows, head_dim):
    count = 2 * mine.shape[0]
    features = mine.shape[1] - 2 * LANES
    half = flat.shape[0]
    core = lax.axis_index("core")
    values = jnp.concatenate([mine[:, :features], peer[:, :features]], axis=0)
    level = jnp.concatenate(
        [mine[:, features : features + LANES], peer[:, features : features + LANES]], axis=0
    )
    owners = jnp.concatenate([mine[:, features + LANES :], peer[:, features + LANES :]], axis=0)
    square = (count, count)
    owner_column = owners[:, :1]
    owner_row = jnp.sum(
        jnp.where(iota(square, 0) == iota(square, 1), owner_column, 0.0), axis=0, keepdims=True
    )
    same = owner_column == owner_row
    peak = jnp.full(level.shape, FLOOR, F32)
    for j in range(count):
        peak = jnp.maximum(
            peak, jnp.where(owners == owners[j : j + 1], level[j : j + 1], FLOOR)
        )
    weight = jnp.exp(level - peak)
    same_table = same.astype(BF16)
    high, low = pieces(weight)
    total = dot(same_table, high) + dot(same_table, low)
    joined = jnp.where(iota(level.shape, 1) < HEADS, peak + jnp.log(total), 0.0)
    heads = head_rows(features, head_dim)
    high, low = pieces(weight / total)
    scaled = values * (dot(high, heads) + dot(low, heads))
    first = (
        jnp.sum(
            jnp.where(same & (iota(square, 0) < iota(square, 1)), 1.0, 0.0), axis=0, keepdims=True
        )
        == 0.0
    )
    owner_row = owner_row.astype(jnp.int32)
    home = owner_row // rows
    place = jnp.where(home % CORES == core, (home // CORES) * rows + owner_row % rows, -1)
    chosen = iota((half, count), 0) == place
    table = chosen.astype(BF16)
    high, low = pieces(scaled)
    flat[:, :features] = dot(table, high) + dot(table, low)
    one = joined.astype(BF16)
    rest = joined - one.astype(F32)
    two = rest.astype(BF16)
    three = (rest - two.astype(F32)).astype(BF16)
    packed = (
        one.astype(F32)
        + pltpu.roll(two.astype(F32), HEADS, 1)
        + pltpu.roll(three.astype(F32), 2 * HEADS, 1)
    ).astype(BF16)
    first_table = (chosen & first).astype(BF16)
    stats = dot(first_table, packed)
    absent = jnp.sum(table.astype(F32), axis=1, keepdims=True) == 0.0
    flat[:, features:] = jnp.where(absent & (iota(stats.shape, 1) < HEADS), FLOOR, stats)
    for n in range(out.shape[0]):
        out[n] = flat[n * rows : (n + 1) * rows, :].astype(BF16)


def project_kernel(parts_in, inputs, w_out, gain, mixed_out, sent, got, *, rows, head_dim):
    half = got.shape[0]
    for n in range(parts_in.shape[0]):
        got[n * rows : (n + 1) * rows, :] = parts_in[n].astype(F32)
    features = w_out.shape[0]
    sub = SUB
    parts = half // sub
    stats = got[:, features:]
    level = stats + pltpu.roll(stats, LANES - HEADS, 1) + pltpu.roll(stats, LANES - 2 * HEADS, 1)
    level = jnp.where(iota(level.shape, 1) < HEADS, level, FLOOR)
    level = level.reshape(parts, sub, LANES)
    peak = jnp.max(level, axis=0)
    peak = jnp.maximum(peak, pltpu.roll(peak, rows, 0))
    weight = jnp.exp(level - peak[None])
    total = jnp.sum(weight, axis=0)
    total = total + pltpu.roll(total, rows, 0)
    weight = (weight / total[None]).reshape(half, LANES)
    heads = head_rows(features, head_dim)
    high, low = pieces(weight)
    spread = dot(high, heads) + dot(low, heads)
    scaled = got[:, :features] * spread
    weighted = jnp.sum(scaled.reshape(parts, sub, features), axis=0)
    context = (weighted + pltpu.roll(weighted, rows, 0)).astype(BF16)
    mixed = inputs[...] + dot(context, w_out[...])
    width = features // SUB
    for j in range(SUB):
        mixed_out[:, j, :] = mixed[:, j * width : (j + 1) * width]
    normed = rms_scaled(mixed, gain[...]).astype(F32)
    sent[...] = jnp.concatenate([normed] * (sent.shape[0] // sub), axis=0).astype(BF16)


def hidden_kernel(part, mixed, *refs, rows):
    *weights, out, held, held_down, tiles, sems = refs
    units = weights[0].shape[0] // 3
    total = held_down.shape[0]
    first, last = [], []
    for n, weight in enumerate(weights):
        for k in range(2):
            target = held.at[pl.ds(k * total + n * units, units)]
            first.append(pltpu.make_async_copy(weight.at[pl.ds(k * units, units)], target, sems.at[3 * n + k]))
        target = held_down.at[pl.ds(n * units, units)]
        last.append(pltpu.make_async_copy(weight.at[pl.ds(2 * units, units)], target, sems.at[3 * n + 2]))
    for copy in first + last:
        copy.start()
    count = part.shape[0]
    line = iota((count, count), 0)
    per = count // rows
    order = (iota((count, count), 1) == (line % per) * rows + line // per).astype(BF16)
    inputs = dot(order, part[...]).astype(BF16)
    for copy in first:
        copy.wait()
    both = lax.dot_general(
        inputs, held[...], (((1,), (1,)), ((), ())), preferred_element_type=F32
    )
    gate = both[:, :total]
    hidden = (gate / (1.0 + jnp.exp(-gate)) * both[:, total:]).astype(BF16)
    for copy in last:
        copy.wait()
    result = dot(hidden, held_down[...])
    width = result.shape[1] // SUB
    for j in range(SUB):
        tiles[:, j, :] = result[:, j * width : (j + 1) * width]
    z = lax.axis_index("z")
    for i in range(rows):
        tiles[i * per + z] = tiles[i * per + z] + mixed[i]
    out[...] = tiles[...].astype(BF16)


def call(kernel, out_shape, args, smem=0, hbm=(), out_specs=None, scratch=(), limit=12 << 20, cost=None):
    vmem = pl.BlockSpec(memory_space=pltpu.VMEM)
    scalar = pl.BlockSpec(memory_space=pltpu.SMEM)
    specs = [scalar] * smem + [vmem] * (len(args) - smem)
    args = list(args)
    for i in hbm:
        specs[i] = pl.BlockSpec(memory_space=pltpu.HBM)
        args[i] = pltpu.with_memory_space_constraint(args[i], pltpu.HBM)
    return pl.pallas_call(
        kernel,
        out_shape=out_shape,
        in_specs=specs,
        out_specs=jax.tree.map(lambda _: vmem, out_shape) if out_specs is None else out_specs,
        scratch_shapes=scratch,
        compiler_params=pltpu.CompilerParams(vmem_limit_bytes=limit),
        cost_estimate=cost,
    )(*args)


def body(
    tokens, attn_gain, w_qkv, w_out, mlp_gain, w_gate_up, w_down, kv_cache, block_owner, block_fill
):
    groups = lax.axis_size("grp")
    z_chips = lax.axis_size("z")
    x_chips = lax.axis_size("x")
    chips = z_chips * x_chips
    rows, features = tokens.shape
    head_dim = features // HEADS
    blocks = kv_cache.shape[0]
    units = w_down.shape[0]
    half = rows * chips
    count = blocks + rows
    width = features // SUB
    swap = [(0, 1), (1, 0)]
    every = ("grp",) + CHIP
    sizes = dict(rows=rows, chips=chips)

    def shape(kind, *dims):
        return jax.ShapeDtypeStruct(dims, kind)

    def tiles(n):
        return pltpu.VMEM((n, SUB, width), F32)

    sent, packed = call(
        lambda *refs: spread_kernel(*refs, chips=chips),
        (shape(BF16, groups * chips, SUB, width), shape(BF16, 3 * units, features)),
        (tokens, jnp.swapaxes(w_gate_up, 1, 2), w_down),
        hbm=(0, 1, 2),
        scratch=[pltpu.VMEM((rows, features), BF16), tiles(rows), pltpu.SemaphoreType.DMA((4,))],
        cost=pl.CostEstimate(flops=10**11, transcendentals=0, bytes_accessed=1 << 18),
    )
    weights = [packed] + [
        lax.ppermute(packed, "x", [(i, (i + k) % x_chips) for i in range(x_chips)])
        for k in range(1, x_chips)
    ]
    got = lax.all_to_all(sent, every, 0, 0, tiled=True)
    peer = lax.ppermute(got, "core", swap)
    weights = weights + [lax.ppermute(weight, "core", swap) for weight in weights]
    gain = attn_gain.reshape(1, features)
    own, inputs = call(
        lambda *refs: own_kernel(*refs, head_dim=head_dim, **sizes),
        (shape(F32, SUB, features + 2 * LANES), shape(F32, SUB, features)),
        (got, gain, w_qkv),
        scratch=[tiles(SUB)],
        cost=pl.CostEstimate(flops=1, transcendentals=0, bytes_accessed=1),
    )
    partial = call(
        lambda *refs: attend_kernel(*refs, head_dim=head_dim, **sizes),
        shape(F32, count, features + 2 * LANES),
        (block_owner, block_fill, got, peer, own, gain, w_qkv, kv_cache),
        smem=2,
        scratch=[tiles(blocks)],
    )
    partial_peer = lax.ppermute(partial, "core", swap)
    sent = call(
        lambda *refs: merge_kernel(*refs, rows=rows, head_dim=head_dim),
        shape(BF16, chips, rows, features + LANES),
        (partial, partial_peer),
        scratch=[pltpu.VMEM((half, features + LANES), F32)],
    )
    got = lax.all_to_all(sent, CHIP, 0, 0, tiled=True)
    mixed, sent = call(
        lambda *refs: project_kernel(*refs, rows=rows, head_dim=head_dim),
        (shape(F32, SUB, SUB, width), shape(BF16, rows * z_chips, features)),
        (got, inputs, w_out, mlp_gain.reshape(1, features)),
        scratch=[pltpu.VMEM((half, features + LANES), F32)],
    )
    got = lax.all_to_all(sent, "z", 0, 0, tiled=True)
    sent = call(
        lambda *refs: hidden_kernel(*refs, rows=rows),
        shape(BF16, rows * z_chips, SUB, width),
        [got, mixed] + weights,
        hbm=range(2, 2 + len(weights)),
        scratch=[
            pltpu.VMEM((2 * len(weights) * units, features), BF16),
            pltpu.VMEM((len(weights) * units, features), BF16),
            tiles(rows * z_chips),
            pltpu.SemaphoreType.DMA((3 * len(weights),)),
        ],
    )
    got = lax.all_to_all(sent, ("grp", "z"), 0, 0, tiled=True)
    return call(
        finish_kernel,
        shape(BF16, rows, features),
        (got,),
        scratch=[tiles(rows)],
    )


def solution(mesh):
    groups, shards = mesh.devices.shape
    devices = mesh.devices.reshape(groups, -1, X_CHIPS, CORES)
    fine = Mesh(devices, ("grp",) + CHIP + ("core",))
    seq = CHIP + ("core",)
    whole = ("grp",) + seq
    in_specs = (
        P(whole, None),
        P(),
        P(),
        P(),
        P(),
        P(None, None, seq),
        P(seq, None),
        P(whole, None, None, None),
        P(whole),
        P(whole),
    )
    return jax.shard_map(
        body, mesh=fine, in_specs=in_specs, out_specs=P(whole, None), check_vma=False
    )
```

```python
import jax
import jax.numpy as jnp
from jax import lax
from jax.experimental import pallas as pl
from jax.experimental.pallas import tpu as pltpu
from jax.sharding import Mesh, PartitionSpec as P

HEADS = 16
CORES = 2
X_CHIPS = 4
LANES = 128
SUB = 8
FLOOR = -1e30
EPSILON = 1e-05
CHIP = ("z", "x")
F32 = jnp.float32
BF16 = jnp.bfloat16


def iota(shape, dim):
    return lax.broadcasted_iota(jnp.int32, shape, dim)


def dot(a, b):
    return jnp.dot(a, b, preferred_element_type=F32)


def pieces(v):
    high = v.astype(BF16)
    return high, (v - high.astype(F32)).astype(BF16)


def head_rows(feature_count, head_dim):
    shape = (LANES, feature_count)
    return (iota(shape, 1) // head_dim == iota(shape, 0)).astype(BF16)


def lay_flat(tiles):
    return jnp.concatenate([tiles[:, j, :] for j in range(SUB)], axis=1)


def spread_kernel(tokens, w_gate_up, w_down, out, packed, held, tiles, sems, *, chips):
    rows, features = tokens.shape
    width = features // SUB
    units = w_down.shape[0]
    copies = [
        pltpu.make_async_copy(w_gate_up.at[0], packed.at[pl.ds(0, units)], sems.at[0]),
        pltpu.make_async_copy(w_gate_up.at[1], packed.at[pl.ds(units, units)], sems.at[1]),
        pltpu.make_async_copy(w_down, packed.at[pl.ds(2 * units, units)], sems.at[2]),
    ]
    first = pltpu.make_async_copy(tokens, held, sems.at[3])
    first.start()
    for copy in copies:
        copy.start()
    first.wait()
    values = held[...].astype(F32)
    for j in range(SUB):
        tiles[:, j, :] = values[:, j * width : (j + 1) * width]
    for g in range(rows):
        row = tiles[g].astype(BF16)
        out[g * chips : (g + 1) * chips] = jnp.broadcast_to(row[None], (chips,) + row.shape)
    for copy in copies:
        copy.wait()


def finish_kernel(got, out, tiles):
    rows = out.shape[0]
    sources = got.shape[0] // rows
    for g in range(rows):
        tiles[g] = jnp.sum(got[g * sources : (g + 1) * sources].astype(F32), axis=0)
    out[...] = lay_flat(tiles).astype(BF16)


def rms_scaled(values, gain):
    scale = lax.rsqrt(jnp.mean(values * values, axis=1, keepdims=True) + EPSILON)
    return (values * scale * gain).astype(BF16)


def own_kernel(got, gain, w_qkv, rows_out, own_out, tiles, *, rows, chips, head_dim):
    core = lax.axis_index("core")
    chip = lax.axis_index(CHIP)
    for k in range(SUB):
        tiles[k] = got[(k % rows) * chips + chip].astype(F32)
    inputs = lay_flat(tiles)
    own_out[...] = inputs
    features = inputs.shape[1]
    qkv = dot(rms_scaled(inputs, gain[...]), w_qkv[...]).astype(BF16).astype(F32)
    query = qkv[:, :features]
    key_new = qkv[:, features : 2 * features]
    shape = (features, LANES)
    by_head = (iota(shape, 0) // head_dim == iota(shape, 1)).astype(BF16)
    high, low = pieces(query * key_new)
    rows_out[:, :features] = qkv[:, 2 * features :]
    rows_out[:, features : features + LANES] = (dot(high, by_head) + dot(low, by_head)) * (
        head_dim**-0.5
    )
    owners = (chip * CORES + core) * rows + iota((SUB, LANES), 0) % rows
    rows_out[:, features + LANES :] = owners.astype(F32)


def attend_kernel(
    owner, fill, got, peer, gain, w_qkv, kv, rows_out, tiles, *, rows, chips, head_dim
):
    blocks, _, span, features = kv.shape
    core = lax.axis_index("core")
    owner_line = iota((blocks, LANES), 0)
    owners = jnp.zeros((blocks, LANES), jnp.int32)
    for b in range(blocks):
        u = owner[b]
        s = u // rows
        at = (u % rows) * chips + s // CORES
        tiles[b] = jnp.where(s % CORES == core, got[at].astype(F32), peer[at].astype(F32))
        owners = jnp.where(owner_line == b, u, owners)
    inputs = lay_flat(tiles)
    query = dot(rms_scaled(inputs, gain[...]), w_qkv[:, :features]).astype(BF16).astype(F32)

    head_mask = iota((HEADS, features), 1) // head_dim == iota((HEADS, features), 0)
    spread = jnp.concatenate(
        [
            jnp.where(head_mask, jnp.broadcast_to(query[b : b + 1], (HEADS, features)), 0.0)
            for b in range(blocks)
        ],
        axis=0,
    ).astype(BF16)
    keys = kv[:, 0].reshape(blocks * span, features)
    values = kv[:, 1].reshape(blocks * span, features)
    scores = lax.dot_general(
        spread, keys, (((1,), (1,)), ((), ())), preferred_element_type=F32
    ) * (head_dim**-0.5)
    wide = scores.shape
    column = iota(wide, 1)
    column_block = column // span
    limit = jnp.zeros((1, blocks * span), jnp.int32)
    limit_block = iota(limit.shape, 1) // span
    for b in range(blocks):
        limit = jnp.where(limit_block == b, fill[b], limit)
    live = (column_block == iota(wide, 0) // HEADS) & (column - column_block * span < limit)
    masked = jnp.where(live, scores, FLOOR)
    peak = jnp.max(masked, axis=1, keepdims=True)
    weights = jnp.where(live, jnp.exp(masked - peak), 0.0).astype(BF16)
    total = jnp.sum(weights.astype(F32), axis=1, keepdims=True)
    summed = dot(weights, values)
    alive = total > 0.0
    safe = jnp.where(alive, total, 1.0)
    level = jnp.where(alive, peak + jnp.log(safe), FLOOR)
    summed = summed * (1.0 / safe)
    diagonal = iota((HEADS, LANES), 0) == iota((HEADS, LANES), 1)
    for b in range(blocks):
        part = slice(b * HEADS, (b + 1) * HEADS)
        rows_out[b : b + 1, :features] = jnp.sum(
            jnp.where(head_mask, summed[part], 0.0), axis=0, keepdims=True
        )
        rows_out[b : b + 1, features : features + LANES] = jnp.sum(
            jnp.where(diagonal, level[part], 0.0), axis=0, keepdims=True
        )
    rows_out[:blocks, features + LANES :] = owners.astype(F32)
    spare = (rows_out.shape[0] - blocks, rows_out.shape[1])
    rows_out[blocks:, :] = jnp.where(
        iota(spare, 1) < features, 0.0, jnp.where(iota(spare, 1) < features + LANES, FLOOR, -1.0)
    )


def merge_kernel(mine_in, own, peer, out, flat, mine, *, rows, head_dim):
    last = mine.shape[0] - rows
    mine[...] = mine_in[...]
    mine[last:, :] = own[SUB - rows :, :]
    count = 2 * mine.shape[0]
    features = mine.shape[1] - 2 * LANES
    half = flat.shape[0]
    core = lax.axis_index("core")
    values = jnp.concatenate([mine[:, :features], peer[:, :features]], axis=0)
    level = jnp.concatenate(
        [mine[:, features : features + LANES], peer[:, features : features + LANES]], axis=0
    )
    owners = jnp.concatenate([mine[:, features + LANES :], peer[:, features + LANES :]], axis=0)
    square = (count, count)
    owner_column = owners[:, :1]
    owner_row = jnp.sum(
        jnp.where(iota(square, 0) == iota(square, 1), owner_column, 0.0), axis=0, keepdims=True
    )
    same = owner_column == owner_row
    peak = jnp.full(level.shape, FLOOR, F32)
    for j in range(count):
        peak = jnp.maximum(
            peak, jnp.where(owners == owners[j : j + 1], level[j : j + 1], FLOOR)
        )
    weight = jnp.exp(level - peak)
    same_table = same.astype(BF16)
    high, low = pieces(weight)
    total = dot(same_table, high) + dot(same_table, low)
    joined = jnp.where(iota(level.shape, 1) < HEADS, peak + jnp.log(total), 0.0)
    heads = head_rows(features, head_dim)
    high, low = pieces(weight / total)
    scaled = values * (dot(high, heads) + dot(low, heads))
    first = (
        jnp.sum(
            jnp.where(same & (iota(square, 0) < iota(square, 1)), 1.0, 0.0), axis=0, keepdims=True
        )
        == 0.0
    )
    owner_row = owner_row.astype(jnp.int32)
    home = owner_row // rows
    place = jnp.where(home % CORES == core, (home // CORES) * rows + owner_row % rows, -1)
    chosen = iota((half, count), 0) == place
    table = chosen.astype(BF16)
    high, low = pieces(scaled)
    flat[:, :features] = dot(table, high) + dot(table, low)
    one = joined.astype(BF16)
    rest = joined - one.astype(F32)
    two = rest.astype(BF16)
    three = (rest - two.astype(F32)).astype(BF16)
    packed = (
        one.astype(F32)
        + pltpu.roll(two.astype(F32), HEADS, 1)
        + pltpu.roll(three.astype(F32), 2 * HEADS, 1)
    ).astype(BF16)
    first_table = (chosen & first).astype(BF16)
    stats = dot(first_table, packed)
    absent = jnp.sum(table.astype(F32), axis=1, keepdims=True) == 0.0
    flat[:, features:] = jnp.where(absent & (iota(stats.shape, 1) < HEADS), FLOOR, stats)
    for n in range(out.shape[0]):
        out[n] = flat[n * rows : (n + 1) * rows, :].astype(BF16)


def project_kernel(parts_in, inputs, w_out, gain, mixed_out, sent, got, *, rows, head_dim):
    half = got.shape[0]
    for n in range(parts_in.shape[0]):
        got[n * rows : (n + 1) * rows, :] = parts_in[n].astype(F32)
    features = w_out.shape[0]
    sub = SUB
    parts = half // sub
    stats = got[:, features:]
    level = stats + pltpu.roll(stats, LANES - HEADS, 1) + pltpu.roll(stats, LANES - 2 * HEADS, 1)
    level = jnp.where(iota(level.shape, 1) < HEADS, level, FLOOR)
    level = level.reshape(parts, sub, LANES)
    peak = jnp.max(level, axis=0)
    peak = jnp.maximum(peak, pltpu.roll(peak, rows, 0))
    weight = jnp.exp(level - peak[None])
    total = jnp.sum(weight, axis=0)
    total = total + pltpu.roll(total, rows, 0)
    weight = (weight / total[None]).reshape(half, LANES)
    heads = head_rows(features, head_dim)
    high, low = pieces(weight)
    spread = dot(high, heads) + dot(low, heads)
    scaled = got[:, :features] * spread
    weighted = jnp.sum(scaled.reshape(parts, sub, features), axis=0)
    context = (weighted + pltpu.roll(weighted, rows, 0)).astype(BF16)
    mixed = inputs[...] + dot(context, w_out[...])
    width = features // SUB
    for j in range(SUB):
        mixed_out[:, j, :] = mixed[:, j * width : (j + 1) * width]
    normed = rms_scaled(mixed, gain[...]).astype(F32)
    sent[...] = jnp.concatenate([normed] * (sent.shape[0] // sub), axis=0).astype(BF16)


def hidden_kernel(part, mixed, *refs, rows):
    *weights, out, held, held_down, tiles, sems = refs
    units = weights[0].shape[0] // 3
    total = held_down.shape[0]
    first, last = [], []
    for n, weight in enumerate(weights):
        for k in range(2):
            target = held.at[pl.ds(k * total + n * units, units)]
            first.append(pltpu.make_async_copy(weight.at[pl.ds(k * units, units)], target, sems.at[3 * n + k]))
        target = held_down.at[pl.ds(n * units, units)]
        last.append(pltpu.make_async_copy(weight.at[pl.ds(2 * units, units)], target, sems.at[3 * n + 2]))
    for k in range(2):
        for copy in first[k * len(weights) : (k + 1) * len(weights)]:
            copy.start()
        for copy in last[k * len(weights) // 2 : (k + 1) * len(weights) // 2]:
            copy.start()
    count = part.shape[0]
    line = iota((count, count), 0)
    per = count // rows
    order = (iota((count, count), 1) == (line % per) * rows + line // per).astype(BF16)
    inputs = dot(order, part[...]).astype(BF16)
    result = None
    chunk = total // 2
    for k in range(2):
        lo = k * chunk
        for copy in first[k * len(weights) : (k + 1) * len(weights)]:
            copy.wait()
        gate, up = [
            lax.dot_general(
                inputs, held[at : at + chunk], (((1,), (1,)), ((), ())), preferred_element_type=F32
            )
            for at in (lo, total + lo)
        ]
        hidden = (gate / (1.0 + jnp.exp(-gate)) * up).astype(BF16)
        for copy in last[k * len(weights) // 2 : (k + 1) * len(weights) // 2]:
            copy.wait()
        term = dot(hidden, held_down[lo : lo + chunk])
        result = term if result is None else result + term
    width = result.shape[1] // SUB
    for j in range(SUB):
        tiles[:, j, :] = result[:, j * width : (j + 1) * width]
    z = lax.axis_index("z")
    for i in range(rows):
        tiles[i * per + z] = tiles[i * per + z] + mixed[i]
    out[...] = tiles[...].astype(BF16)


def call(kernel, out_shape, args, smem=0, hbm=(), out_specs=None, scratch=(), limit=12 << 20, cost=None):
    vmem = pl.BlockSpec(memory_space=pltpu.VMEM)
    scalar = pl.BlockSpec(memory_space=pltpu.SMEM)
    specs = [scalar] * smem + [vmem] * (len(args) - smem)
    args = list(args)
    for i in hbm:
        specs[i] = pl.BlockSpec(memory_space=pltpu.HBM)
        args[i] = pltpu.with_memory_space_constraint(args[i], pltpu.HBM)
    return pl.pallas_call(
        kernel,
        out_shape=out_shape,
        in_specs=specs,
        out_specs=jax.tree.map(lambda _: vmem, out_shape) if out_specs is None else out_specs,
        scratch_shapes=scratch,
        compiler_params=pltpu.CompilerParams(vmem_limit_bytes=limit),
        cost_estimate=cost,
    )(*args)


def body(
    tokens, attn_gain, w_qkv, w_out, mlp_gain, w_gate_up, w_down, kv_cache, block_owner, block_fill
):
    groups = lax.axis_size("grp")
    z_chips = lax.axis_size("z")
    x_chips = lax.axis_size("x")
    chips = z_chips * x_chips
    rows, features = tokens.shape
    head_dim = features // HEADS
    blocks = kv_cache.shape[0]
    units = w_down.shape[0]
    half = rows * chips
    count = blocks + rows
    width = features // SUB
    swap = [(0, 1), (1, 0)]
    every = ("grp",) + CHIP
    sizes = dict(rows=rows, chips=chips)

    def shape(kind, *dims):
        return jax.ShapeDtypeStruct(dims, kind)

    def tiles(n):
        return pltpu.VMEM((n, SUB, width), F32)

    sent, packed = call(
        lambda *refs: spread_kernel(*refs, chips=chips),
        (shape(BF16, groups * chips, SUB, width), shape(BF16, 3 * units, features)),
        (tokens, jnp.swapaxes(w_gate_up, 1, 2), w_down),
        hbm=(0, 1, 2),
        scratch=[pltpu.VMEM((rows, features), BF16), tiles(rows), pltpu.SemaphoreType.DMA((4,))],
        cost=pl.CostEstimate(flops=10**11, transcendentals=0, bytes_accessed=1 << 18),
    )
    weights = [packed] + [
        lax.ppermute(packed, "x", [(i, (i + k) % x_chips) for i in range(x_chips)])
        for k in range(1, x_chips)
    ]
    got = lax.all_to_all(sent, every, 0, 0, tiled=True)
    peer = lax.ppermute(got, "core", swap)
    weights = weights + [lax.ppermute(weight, "core", swap) for weight in weights]
    gain = attn_gain.reshape(1, features)
    partial = call(
        lambda *refs: attend_kernel(*refs, head_dim=head_dim, **sizes),
        shape(F32, count, features + 2 * LANES),
        (block_owner, block_fill, got, peer, gain, w_qkv, kv_cache),
        smem=2,
        scratch=[tiles(blocks)],
    )
    got, partial = lax.optimization_barrier((got, partial))
    partial_peer = lax.ppermute(partial, "core", swap)
    own, inputs = call(
        lambda *refs: own_kernel(*refs, head_dim=head_dim, **sizes),
        (shape(F32, SUB, features + 2 * LANES), shape(F32, SUB, features)),
        (got, gain, w_qkv),
        scratch=[tiles(SUB)],
        cost=pl.CostEstimate(flops=1, transcendentals=0, bytes_accessed=1),
    )
    sent = call(
        lambda *refs: merge_kernel(*refs, rows=rows, head_dim=head_dim),
        shape(BF16, chips, rows, features + LANES),
        (partial, own, partial_peer),
        scratch=[
            pltpu.VMEM((half, features + LANES), F32),
            pltpu.VMEM((count, features + 2 * LANES), F32),
        ],
    )
    got = lax.all_to_all(sent, CHIP, 0, 0, tiled=True)
    mixed, sent = call(
        lambda *refs: project_kernel(*refs, rows=rows, head_dim=head_dim),
        (shape(F32, SUB, SUB, width), shape(BF16, rows * z_chips, features)),
        (got, inputs, w_out, mlp_gain.reshape(1, features)),
        scratch=[pltpu.VMEM((half, features + LANES), F32)],
    )
    got = lax.all_to_all(sent, "z", 0, 0, tiled=True)
    sent = call(
        lambda *refs: hidden_kernel(*refs, rows=rows),
        shape(BF16, rows * z_chips, SUB, width),
        [got, mixed] + weights,
        hbm=range(2, 2 + len(weights)),
        scratch=[
            pltpu.VMEM((2 * len(weights) * units, features), BF16),
            pltpu.VMEM((len(weights) * units, features), BF16),
            tiles(rows * z_chips),
            pltpu.SemaphoreType.DMA((3 * len(weights),)),
        ],
    )
    got = lax.all_to_all(sent, ("grp", "z"), 0, 0, tiled=True)
    return call(
        finish_kernel,
        shape(BF16, rows, features),
        (got,),
        scratch=[tiles(rows)],
    )


def solution(mesh):
    groups, shards = mesh.devices.shape
    devices = mesh.devices.reshape(groups, -1, X_CHIPS, CORES)
    fine = Mesh(devices, ("grp",) + CHIP + ("core",))
    seq = CHIP + ("core",)
    whole = ("grp",) + seq
    in_specs = (
        P(whole, None),
        P(),
        P(),
        P(),
        P(),
        P(None, None, seq),
        P(seq, None),
        P(whole, None, None, None),
        P(whole),
        P(whole),
    )
    return jax.shard_map(
        body, mesh=fine, in_specs=in_specs, out_specs=P(whole, None), check_vma=False
    )
```

```python
import jax
import jax.numpy as jnp
from jax import lax
from jax.experimental import pallas as pl
from jax.experimental.pallas import tpu as pltpu
from jax.sharding import Mesh, PartitionSpec as P

HEADS = 16
CORES = 2
X_CHIPS = 4
LANES = 128
SUB = 8
FLOOR = -1e30
EPSILON = 1e-05
CHIP = ("z", "x")
F32 = jnp.float32
BF16 = jnp.bfloat16


def iota(shape, dim):
    return lax.broadcasted_iota(jnp.int32, shape, dim)


def dot(a, b):
    return jnp.dot(a, b, preferred_element_type=F32)


def pieces(v):
    high = v.astype(BF16)
    return high, (v - high.astype(F32)).astype(BF16)


def head_rows(feature_count, head_dim):
    shape = (LANES, feature_count)
    return (iota(shape, 1) // head_dim == iota(shape, 0)).astype(BF16)


def lay_flat(tiles):
    return jnp.concatenate([tiles[:, j, :] for j in range(SUB)], axis=1)


def spread_kernel(tokens, w_gate_up, w_down, out, packed, held, tiles, sems, *, chips):
    rows, features = tokens.shape
    width = features // SUB
    units = w_down.shape[0]
    copies = [
        pltpu.make_async_copy(w_gate_up.at[0], packed.at[pl.ds(0, units)], sems.at[0]),
        pltpu.make_async_copy(w_gate_up.at[1], packed.at[pl.ds(units, units)], sems.at[1]),
        pltpu.make_async_copy(w_down, packed.at[pl.ds(2 * units, units)], sems.at[2]),
    ]
    first = pltpu.make_async_copy(tokens, held, sems.at[3])
    first.start()
    for copy in copies:
        copy.start()
    first.wait()
    values = held[...].astype(F32)
    for j in range(SUB):
        tiles[:, j, :] = values[:, j * width : (j + 1) * width]
    for g in range(rows):
        row = tiles[g].astype(BF16)
        out[g * chips : (g + 1) * chips] = jnp.broadcast_to(row[None], (chips,) + row.shape)
    for copy in copies:
        copy.wait()


def finish_kernel(got, out, tiles):
    rows = out.shape[0]
    sources = got.shape[0] // rows
    for g in range(rows):
        tiles[g] = jnp.sum(got[g * sources : (g + 1) * sources].astype(F32), axis=0)
    out[...] = lay_flat(tiles).astype(BF16)


def rms_scaled(values, gain):
    scale = lax.rsqrt(jnp.mean(values * values, axis=1, keepdims=True) + EPSILON)
    return (values * scale * gain).astype(BF16)


def own_kernel(got, gain, w_qkv, rows_out, own_out, tiles, *, rows, chips, head_dim):
    core = lax.axis_index("core")
    chip = lax.axis_index(CHIP)
    for k in range(SUB):
        tiles[k] = got[(k % rows) * chips + chip].astype(F32)
    inputs = lay_flat(tiles)
    own_out[...] = inputs
    features = inputs.shape[1]
    qkv = dot(rms_scaled(inputs, gain[...]), w_qkv[...]).astype(BF16).astype(F32)
    query = qkv[:, :features]
    key_new = qkv[:, features : 2 * features]
    shape = (features, LANES)
    by_head = (iota(shape, 0) // head_dim == iota(shape, 1)).astype(BF16)
    high, low = pieces(query * key_new)
    rows_out[:, :features] = qkv[:, 2 * features :]
    rows_out[:, features : features + LANES] = (dot(high, by_head) + dot(low, by_head)) * (
        head_dim**-0.5
    )
    owners = (chip * CORES + core) * rows + iota((SUB, LANES), 0) % rows
    rows_out[:, features + LANES :] = owners.astype(F32)


def attend_kernel(
    owner, fill, got, peer, gain, w_qkv, kv, rows_out, tiles, *, rows, chips, head_dim
):
    blocks, _, span, features = kv.shape
    core = lax.axis_index("core")
    owner_line = iota((blocks, LANES), 0)
    owners = jnp.zeros((blocks, LANES), jnp.int32)
    for b in range(blocks):
        u = owner[b]
        s = u // rows
        at = (u % rows) * chips + s // CORES
        tiles[b] = jnp.where(s % CORES == core, got[at].astype(F32), peer[at].astype(F32))
        owners = jnp.where(owner_line == b, u, owners)
    inputs = lay_flat(tiles)
    query = dot(rms_scaled(inputs, gain[...]), w_qkv[:, :features]).astype(BF16).astype(F32)

    head_mask = iota((HEADS, features), 1) // head_dim == iota((HEADS, features), 0)
    diagonal = iota((HEADS, LANES), 0) == iota((HEADS, LANES), 1)
    nt = (((1,), (1,)), ((), ()))
    scores = []
    for b in range(blocks):
        row = jnp.broadcast_to(query[b : b + 1], (HEADS, features))
        spread = jnp.where(head_mask, row, 0.0).astype(BF16)
        scores.append(lax.dot_general(spread, kv[b, 0], nt, preferred_element_type=F32))
    column = iota((HEADS, span), 1)
    for b in range(blocks):
        live = column < fill[b]
        masked = jnp.where(live, scores[b] * (head_dim**-0.5), FLOOR)
        peak = jnp.max(masked, axis=1, keepdims=True)
        weights = jnp.where(live, jnp.exp(masked - peak), 0.0).astype(BF16)
        total = jnp.sum(weights.astype(F32), axis=1, keepdims=True)
        summed = dot(weights, kv[b, 1])
        alive = total > 0.0
        safe = jnp.where(alive, total, 1.0)
        level = jnp.where(alive, peak + jnp.log(safe), FLOOR)
        summed = summed * (1.0 / safe)
        rows_out[b : b + 1, :features] = jnp.sum(
            jnp.where(head_mask, summed, 0.0), axis=0, keepdims=True
        )
        rows_out[b : b + 1, features : features + LANES] = jnp.sum(
            jnp.where(diagonal, level, 0.0), axis=0, keepdims=True
        )
    rows_out[:blocks, features + LANES :] = owners.astype(F32)
    spare = (rows_out.shape[0] - blocks, rows_out.shape[1])
    rows_out[blocks:, :] = jnp.where(
        iota(spare, 1) < features, 0.0, jnp.where(iota(spare, 1) < features + LANES, FLOOR, -1.0)
    )


def merge_kernel(mine_in, own, peer, out, flat, mine, *, rows, head_dim):
    last = mine.shape[0] - rows
    mine[...] = mine_in[...]
    mine[last:, :] = own[SUB - rows :, :]
    count = 2 * mine.shape[0]
    features = mine.shape[1] - 2 * LANES
    half = flat.shape[0]
    core = lax.axis_index("core")
    values = jnp.concatenate([mine[:, :features], peer[:, :features]], axis=0)
    level = jnp.concatenate(
        [mine[:, features : features + LANES], peer[:, features : features + LANES]], axis=0
    )
    owners = jnp.concatenate([mine[:, features + LANES :], peer[:, features + LANES :]], axis=0)
    square = (count, count)
    owner_column = owners[:, :1]
    owner_row = jnp.sum(
        jnp.where(iota(square, 0) == iota(square, 1), owner_column, 0.0), axis=0, keepdims=True
    )
    same = owner_column == owner_row
    peak = jnp.full(level.shape, FLOOR, F32)
    for j in range(count):
        peak = jnp.maximum(
            peak, jnp.where(owners == owners[j : j + 1], level[j : j + 1], FLOOR)
        )
    weight = jnp.exp(level - peak)
    same_table = same.astype(BF16)
    high, low = pieces(weight)
    total = dot(same_table, high) + dot(same_table, low)
    joined = jnp.where(iota(level.shape, 1) < HEADS, peak + jnp.log(total), 0.0)
    heads = head_rows(features, head_dim)
    high, low = pieces(weight / total)
    scaled = values * (dot(high, heads) + dot(low, heads))
    first = (
        jnp.sum(
            jnp.where(same & (iota(square, 0) < iota(square, 1)), 1.0, 0.0), axis=0, keepdims=True
        )
        == 0.0
    )
    owner_row = owner_row.astype(jnp.int32)
    home = owner_row // rows
    place = jnp.where(home % CORES == core, (home // CORES) * rows + owner_row % rows, -1)
    chosen = iota((half, count), 0) == place
    table = chosen.astype(BF16)
    high, low = pieces(scaled)
    flat[:, :features] = dot(table, high) + dot(table, low)
    one = joined.astype(BF16)
    rest = joined - one.astype(F32)
    two = rest.astype(BF16)
    three = (rest - two.astype(F32)).astype(BF16)
    packed = (
        one.astype(F32)
        + pltpu.roll(two.astype(F32), HEADS, 1)
        + pltpu.roll(three.astype(F32), 2 * HEADS, 1)
    ).astype(BF16)
    first_table = (chosen & first).astype(BF16)
    stats = dot(first_table, packed)
    absent = jnp.sum(table.astype(F32), axis=1, keepdims=True) == 0.0
    flat[:, features:] = jnp.where(absent & (iota(stats.shape, 1) < HEADS), FLOOR, stats)
    for n in range(out.shape[0]):
        out[n] = flat[n * rows : (n + 1) * rows, :].astype(BF16)


def project_kernel(parts_in, inputs, w_out, gain, mixed_out, sent, got, *, rows, head_dim):
    half = got.shape[0]
    for n in range(parts_in.shape[0]):
        got[n * rows : (n + 1) * rows, :] = parts_in[n].astype(F32)
    features = w_out.shape[0]
    sub = SUB
    parts = half // sub
    stats = got[:, features:]
    level = stats + pltpu.roll(stats, LANES - HEADS, 1) + pltpu.roll(stats, LANES - 2 * HEADS, 1)
    level = jnp.where(iota(level.shape, 1) < HEADS, level, FLOOR)
    level = level.reshape(parts, sub, LANES)
    peak = jnp.max(level, axis=0)
    peak = jnp.maximum(peak, pltpu.roll(peak, rows, 0))
    weight = jnp.exp(level - peak[None])
    total = jnp.sum(weight, axis=0)
    total = total + pltpu.roll(total, rows, 0)
    weight = (weight / total[None]).reshape(half, LANES)
    heads = head_rows(features, head_dim)
    high, low = pieces(weight)
    spread = dot(high, heads) + dot(low, heads)
    scaled = got[:, :features] * spread
    weighted = jnp.sum(scaled.reshape(parts, sub, features), axis=0)
    context = (weighted + pltpu.roll(weighted, rows, 0)).astype(BF16)
    mixed = inputs[...] + dot(context, w_out[...])
    width = features // SUB
    for j in range(SUB):
        mixed_out[:, j, :] = mixed[:, j * width : (j + 1) * width]
    normed = rms_scaled(mixed, gain[...]).astype(F32)
    sent[...] = jnp.concatenate([normed] * (sent.shape[0] // sub), axis=0).astype(BF16)


def hidden_kernel(part, mixed, *refs, rows):
    *weights, out, held, held_down, tiles, sems = refs
    units = weights[0].shape[0] // 3
    total = held_down.shape[0]
    first, last = [], []
    for n, weight in enumerate(weights):
        for k in range(2):
            target = held.at[pl.ds(k * total + n * units, units)]
            first.append(pltpu.make_async_copy(weight.at[pl.ds(k * units, units)], target, sems.at[3 * n + k]))
        target = held_down.at[pl.ds(n * units, units)]
        last.append(pltpu.make_async_copy(weight.at[pl.ds(2 * units, units)], target, sems.at[3 * n + 2]))
    for k in range(2):
        for copy in first[k * len(weights) : (k + 1) * len(weights)]:
            copy.start()
        for copy in last[k * len(weights) // 2 : (k + 1) * len(weights) // 2]:
            copy.start()
    count = part.shape[0]
    line = iota((count, count), 0)
    per = count // rows
    order = (iota((count, count), 1) == (line % per) * rows + line // per).astype(BF16)
    inputs = dot(order, part[...]).astype(BF16)
    result = None
    chunk = total // 2
    for k in range(2):
        lo = k * chunk
        for copy in first[k * len(weights) : (k + 1) * len(weights)]:
            copy.wait()
        gate, up = [
            lax.dot_general(
                inputs, held[at : at + chunk], (((1,), (1,)), ((), ())), preferred_element_type=F32
            )
            for at in (lo, total + lo)
        ]
        hidden = (gate / (1.0 + jnp.exp(-gate)) * up).astype(BF16)
        for copy in last[k * len(weights) // 2 : (k + 1) * len(weights) // 2]:
            copy.wait()
        term = dot(hidden, held_down[lo : lo + chunk])
        result = term if result is None else result + term
    width = result.shape[1] // SUB
    for j in range(SUB):
        tiles[:, j, :] = result[:, j * width : (j + 1) * width]
    z = lax.axis_index("z")
    for i in range(rows):
        tiles[i * per + z] = tiles[i * per + z] + mixed[i]
    out[...] = tiles[...].astype(BF16)


def call(kernel, out_shape, args, smem=0, hbm=(), out_specs=None, scratch=(), limit=12 << 20, cost=None):
    vmem = pl.BlockSpec(memory_space=pltpu.VMEM)
    scalar = pl.BlockSpec(memory_space=pltpu.SMEM)
    specs = [scalar] * smem + [vmem] * (len(args) - smem)
    args = list(args)
    for i in hbm:
        specs[i] = pl.BlockSpec(memory_space=pltpu.HBM)
        args[i] = pltpu.with_memory_space_constraint(args[i], pltpu.HBM)
    return pl.pallas_call(
        kernel,
        out_shape=out_shape,
        in_specs=specs,
        out_specs=jax.tree.map(lambda _: vmem, out_shape) if out_specs is None else out_specs,
        scratch_shapes=scratch,
        compiler_params=pltpu.CompilerParams(vmem_limit_bytes=limit),
        cost_estimate=cost,
    )(*args)


def body(
    tokens, attn_gain, w_qkv, w_out, mlp_gain, w_gate_up, w_down, kv_cache, block_owner, block_fill
):
    groups = lax.axis_size("grp")
    z_chips = lax.axis_size("z")
    x_chips = lax.axis_size("x")
    chips = z_chips * x_chips
    rows, features = tokens.shape
    head_dim = features // HEADS
    blocks = kv_cache.shape[0]
    units = w_down.shape[0]
    half = rows * chips
    count = blocks + rows
    width = features // SUB
    swap = [(0, 1), (1, 0)]
    every = ("grp",) + CHIP
    sizes = dict(rows=rows, chips=chips)

    def shape(kind, *dims):
        return jax.ShapeDtypeStruct(dims, kind)

    def tiles(n):
        return pltpu.VMEM((n, SUB, width), F32)

    sent, packed = call(
        lambda *refs: spread_kernel(*refs, chips=chips),
        (shape(BF16, groups * chips, SUB, width), shape(BF16, 3 * units, features)),
        (tokens, jnp.swapaxes(w_gate_up, 1, 2), w_down),
        hbm=(0, 1, 2),
        scratch=[pltpu.VMEM((rows, features), BF16), tiles(rows), pltpu.SemaphoreType.DMA((4,))],
        cost=pl.CostEstimate(flops=10**11, transcendentals=0, bytes_accessed=1 << 18),
    )
    weights = [packed] + [
        lax.ppermute(packed, "x", [(i, (i + k) % x_chips) for i in range(x_chips)])
        for k in range(1, x_chips)
    ]
    got = lax.all_to_all(sent, every, 0, 0, tiled=True)
    peer = lax.ppermute(got, "core", swap)
    weights = weights + [lax.ppermute(weight, "core", swap) for weight in weights]
    gain = attn_gain.reshape(1, features)
    partial = call(
        lambda *refs: attend_kernel(*refs, head_dim=head_dim, **sizes),
        shape(F32, count, features + 2 * LANES),
        (block_owner, block_fill, got, peer, gain, w_qkv, kv_cache),
        smem=2,
        scratch=[tiles(blocks)],
    )
    got, partial = lax.optimization_barrier((got, partial))
    partial_peer = lax.ppermute(partial, "core", swap)
    own, inputs = call(
        lambda *refs: own_kernel(*refs, head_dim=head_dim, **sizes),
        (shape(F32, SUB, features + 2 * LANES), shape(F32, SUB, features)),
        (got, gain, w_qkv),
        scratch=[tiles(SUB)],
        cost=pl.CostEstimate(flops=1, transcendentals=0, bytes_accessed=1),
    )
    sent = call(
        lambda *refs: merge_kernel(*refs, rows=rows, head_dim=head_dim),
        shape(BF16, chips, rows, features + LANES),
        (partial, own, partial_peer),
        scratch=[
            pltpu.VMEM((half, features + LANES), F32),
            pltpu.VMEM((count, features + 2 * LANES), F32),
        ],
    )
    got = lax.all_to_all(sent, CHIP, 0, 0, tiled=True)
    mixed, sent = call(
        lambda *refs: project_kernel(*refs, rows=rows, head_dim=head_dim),
        (shape(F32, SUB, SUB, width), shape(BF16, rows * z_chips, features)),
        (got, inputs, w_out, mlp_gain.reshape(1, features)),
        scratch=[pltpu.VMEM((half, features + LANES), F32)],
    )
    got = lax.all_to_all(sent, "z", 0, 0, tiled=True)
    sent = call(
        lambda *refs: hidden_kernel(*refs, rows=rows),
        shape(BF16, rows * z_chips, SUB, width),
        [got, mixed] + weights,
        hbm=range(2, 2 + len(weights)),
        scratch=[
            pltpu.VMEM((2 * len(weights) * units, features), BF16),
            pltpu.VMEM((len(weights) * units, features), BF16),
            tiles(rows * z_chips),
            pltpu.SemaphoreType.DMA((3 * len(weights),)),
        ],
    )
    got = lax.all_to_all(sent, ("grp", "z"), 0, 0, tiled=True)
    return call(
        finish_kernel,
        shape(BF16, rows, features),
        (got,),
        scratch=[tiles(rows)],
    )


def solution(mesh):
    groups, shards = mesh.devices.shape
    devices = mesh.devices.reshape(groups, -1, X_CHIPS, CORES)
    fine = Mesh(devices, ("grp",) + CHIP + ("core",))
    seq = CHIP + ("core",)
    whole = ("grp",) + seq
    in_specs = (
        P(whole, None),
        P(),
        P(),
        P(),
        P(),
        P(None, None, seq),
        P(seq, None),
        P(whole, None, None, None),
        P(whole),
        P(whole),
    )
    return jax.shard_map(
        body, mesh=fine, in_specs=in_specs, out_specs=P(whole, None), check_vma=False
    )
```

```python
import jax
import jax.numpy as jnp
from jax import lax
from jax.experimental import pallas as pl
from jax.experimental.pallas import tpu as pltpu
from jax.sharding import Mesh, PartitionSpec as P

HEADS = 16
CORES = 2
X_CHIPS = 4
LANES = 128
SUB = 8
FLOOR = -1e30
EPSILON = 1e-05
CHIP = ("z", "x")
F32 = jnp.float32
BF16 = jnp.bfloat16


def iota(shape, dim):
    return lax.broadcasted_iota(jnp.int32, shape, dim)


def dot(a, b):
    return jnp.dot(a, b, preferred_element_type=F32)


def pieces(v):
    high = v.astype(BF16)
    return high, (v - high.astype(F32)).astype(BF16)


def head_rows(feature_count, head_dim):
    shape = (LANES, feature_count)
    return (iota(shape, 1) // head_dim == iota(shape, 0)).astype(BF16)


def lay_flat(tiles):
    return jnp.concatenate([tiles[:, j, :] for j in range(SUB)], axis=1)


def spread_kernel(tokens, w_gate_up, w_down, out, packed, held, tiles, sems, *, chips):
    rows, features = tokens.shape
    width = features // SUB
    units = w_down.shape[0]
    copies = [
        pltpu.make_async_copy(w_gate_up.at[0], packed.at[pl.ds(0, units)], sems.at[0]),
        pltpu.make_async_copy(w_gate_up.at[1], packed.at[pl.ds(units, units)], sems.at[1]),
        pltpu.make_async_copy(w_down, packed.at[pl.ds(2 * units, units)], sems.at[2]),
    ]
    first = pltpu.make_async_copy(tokens, held, sems.at[3])
    first.start()
    for copy in copies:
        copy.start()
    first.wait()
    values = held[...].astype(F32)
    for j in range(SUB):
        tiles[:, j, :] = values[:, j * width : (j + 1) * width]
    for g in range(rows):
        row = tiles[g].astype(BF16)
        out[g * chips : (g + 1) * chips] = jnp.broadcast_to(row[None], (chips,) + row.shape)
    for copy in copies:
        copy.wait()


def finish_kernel(got, out, tiles):
    rows = out.shape[0]
    sources = got.shape[0] // rows
    for g in range(rows):
        tiles[g] = jnp.sum(got[g * sources : (g + 1) * sources].astype(F32), axis=0)
    out[...] = lay_flat(tiles).astype(BF16)


def rms_scaled(values, gain):
    scale = lax.rsqrt(jnp.mean(values * values, axis=1, keepdims=True) + EPSILON)
    return (values * scale * gain).astype(BF16)


def own_kernel(got, gain, w_qkv, rows_out, own_out, tiles, *, rows, chips, head_dim):
    core = lax.axis_index("core")
    chip = lax.axis_index(CHIP)
    for k in range(SUB):
        tiles[k] = got[(k % rows) * chips + chip].astype(F32)
    inputs = lay_flat(tiles)
    own_out[...] = inputs
    features = inputs.shape[1]
    qkv = dot(rms_scaled(inputs, gain[...]), w_qkv[...]).astype(BF16).astype(F32)
    query = qkv[:, :features]
    key_new = qkv[:, features : 2 * features]
    shape = (features, LANES)
    by_head = (iota(shape, 0) // head_dim == iota(shape, 1)).astype(BF16)
    high, low = pieces(query * key_new)
    rows_out[:, :features] = qkv[:, 2 * features :]
    rows_out[:, features : features + LANES] = (dot(high, by_head) + dot(low, by_head)) * (
        head_dim**-0.5
    )
    owners = (chip * CORES + core) * rows + iota((SUB, LANES), 0) % rows
    rows_out[:, features + LANES :] = owners.astype(F32)


def attend_kernel(
    owner, fill, got, peer, gain, w_qkv, kv, rows_out, tiles, *, rows, chips, head_dim
):
    blocks, _, span, features = kv.shape
    core = lax.axis_index("core")
    owner_line = iota((blocks, LANES), 0)
    owners = jnp.zeros((blocks, LANES), jnp.int32)
    for b in range(blocks):
        u = owner[b]
        s = u // rows
        at = (u % rows) * chips + s // CORES
        tiles[b] = jnp.where(s % CORES == core, got[at].astype(F32), peer[at].astype(F32))
        owners = jnp.where(owner_line == b, u, owners)
    inputs = lay_flat(tiles)
    query = dot(rms_scaled(inputs, gain[...]), w_qkv[:, :features]).astype(BF16).astype(F32)

    head_mask = iota((HEADS, features), 1) // head_dim == iota((HEADS, features), 0)
    diagonal = iota((HEADS, LANES), 0) == iota((HEADS, LANES), 1)
    nt = (((1,), (1,)), ((), ()))
    scores = []
    for b in range(blocks):
        row = jnp.broadcast_to(query[b : b + 1], (HEADS, features))
        spread = jnp.where(head_mask, row, 0.0).astype(BF16)
        scores.append(lax.dot_general(spread, kv[b, 0], nt, preferred_element_type=F32))
    column = iota((HEADS, span), 1)
    for b in range(blocks):
        live = column < fill[b]
        masked = jnp.where(live, scores[b] * (head_dim**-0.5), FLOOR)
        peak = jnp.max(masked, axis=1, keepdims=True)
        weights = jnp.where(live, jnp.exp(masked - peak), 0.0).astype(BF16)
        total = jnp.sum(weights.astype(F32), axis=1, keepdims=True)
        summed = dot(weights, kv[b, 1])
        alive = total > 0.0
        safe = jnp.where(alive, total, 1.0)
        level = jnp.where(alive, peak + jnp.log(safe), FLOOR)
        summed = summed * (1.0 / safe)
        rows_out[b : b + 1, :features] = jnp.sum(
            jnp.where(head_mask, summed, 0.0), axis=0, keepdims=True
        )
        rows_out[b : b + 1, features : features + LANES] = jnp.sum(
            jnp.where(diagonal, level, 0.0), axis=0, keepdims=True
        )
    rows_out[:blocks, features + LANES :] = owners.astype(F32)
    spare = (rows_out.shape[0] - blocks, rows_out.shape[1])
    rows_out[blocks:, :] = jnp.where(
        iota(spare, 1) < features, 0.0, jnp.where(iota(spare, 1) < features + LANES, FLOOR, -1.0)
    )


def merge_kernel(mine_in, own, peer, out, flat, mine, *, rows, head_dim):
    last = mine.shape[0] - rows
    mine[...] = mine_in[...]
    mine[last:, :] = own[SUB - rows :, :]
    count = 2 * mine.shape[0]
    features = mine.shape[1] - 2 * LANES
    half = flat.shape[0]
    core = lax.axis_index("core")
    values = jnp.concatenate([mine[:, :features], peer[:, :features]], axis=0)
    level = jnp.concatenate(
        [mine[:, features : features + LANES], peer[:, features : features + LANES]], axis=0
    )
    owners = jnp.concatenate([mine[:, features + LANES :], peer[:, features + LANES :]], axis=0)
    square = (count, count)
    owner_column = owners[:, :1]
    owner_row = jnp.sum(
        jnp.where(iota(square, 0) == iota(square, 1), owner_column, 0.0), axis=0, keepdims=True
    )
    same = owner_column == owner_row
    peak = jnp.full(level.shape, FLOOR, F32)
    for j in range(count):
        peak = jnp.maximum(
            peak, jnp.where(owners == owners[j : j + 1], level[j : j + 1], FLOOR)
        )
    weight = jnp.exp(level - peak)
    same_table = same.astype(BF16)
    high, low = pieces(weight)
    total = dot(same_table, high) + dot(same_table, low)
    joined = jnp.where(iota(level.shape, 1) < HEADS, peak + jnp.log(total), 0.0)
    heads = head_rows(features, head_dim)
    high, low = pieces(weight / total)
    scaled = values * (dot(high, heads) + dot(low, heads))
    first = (
        jnp.sum(
            jnp.where(same & (iota(square, 0) < iota(square, 1)), 1.0, 0.0), axis=0, keepdims=True
        )
        == 0.0
    )
    owner_row = owner_row.astype(jnp.int32)
    home = owner_row // rows
    place = jnp.where(home % CORES == core, (home // CORES) * rows + owner_row % rows, -1)
    chosen = iota((half, count), 0) == place
    table = chosen.astype(BF16)
    high, low = pieces(scaled)
    flat[:, :features] = dot(table, high) + dot(table, low)
    one = joined.astype(BF16)
    rest = joined - one.astype(F32)
    two = rest.astype(BF16)
    three = (rest - two.astype(F32)).astype(BF16)
    packed = (
        one.astype(F32)
        + pltpu.roll(two.astype(F32), HEADS, 1)
        + pltpu.roll(three.astype(F32), 2 * HEADS, 1)
    ).astype(BF16)
    first_table = (chosen & first).astype(BF16)
    stats = dot(first_table, packed)
    absent = jnp.sum(table.astype(F32), axis=1, keepdims=True) == 0.0
    flat[:, features:] = jnp.where(absent & (iota(stats.shape, 1) < HEADS), FLOOR, stats)
    step = 2 * rows
    for n in range(out.shape[0] // 2):
        pair = flat[n * step : (n + 1) * step, :].astype(BF16)
        out[2 * n] = pair[:rows]
        out[2 * n + 1] = pair[rows:]


def project_kernel(parts_in, inputs, w_out, gain, mixed_out, sent, got, *, rows, head_dim):
    half = got.shape[0]
    for n in range(parts_in.shape[0]):
        got[n * rows : (n + 1) * rows, :] = parts_in[n].astype(F32)
    features = w_out.shape[0]
    sub = SUB
    parts = half // sub
    stats = got[:, features:]
    level = stats + pltpu.roll(stats, LANES - HEADS, 1) + pltpu.roll(stats, LANES - 2 * HEADS, 1)
    level = jnp.where(iota(level.shape, 1) < HEADS, level, FLOOR)
    level = level.reshape(parts, sub, LANES)
    peak = jnp.max(level, axis=0)
    peak = jnp.maximum(peak, pltpu.roll(peak, rows, 0))
    weight = jnp.exp(level - peak[None])
    total = jnp.sum(weight, axis=0)
    total = total + pltpu.roll(total, rows, 0)
    weight = (weight / total[None]).reshape(half, LANES)
    heads = head_rows(features, head_dim)
    high, low = pieces(weight)
    spread = dot(high, heads) + dot(low, heads)
    scaled = got[:, :features] * spread
    weighted = jnp.sum(scaled.reshape(parts, sub, features), axis=0)
    context = (weighted + pltpu.roll(weighted, rows, 0)).astype(BF16)
    mixed = inputs[...] + dot(context, w_out[...])
    width = features // SUB
    for j in range(SUB):
        mixed_out[:, j, :] = mixed[:, j * width : (j + 1) * width]
    normed = rms_scaled(mixed, gain[...]).astype(F32)
    sent[...] = jnp.concatenate([normed] * (sent.shape[0] // sub), axis=0).astype(BF16)


def hidden_kernel(part, mixed, *refs, rows):
    *weights, out, held, held_down, tiles, sems = refs
    units = weights[0].shape[0] // 3
    total = held_down.shape[0]
    first, last = [], []
    for n, weight in enumerate(weights):
        for k in range(2):
            target = held.at[pl.ds(k * total + n * units, units)]
            first.append(pltpu.make_async_copy(weight.at[pl.ds(k * units, units)], target, sems.at[3 * n + k]))
        target = held_down.at[pl.ds(n * units, units)]
        last.append(pltpu.make_async_copy(weight.at[pl.ds(2 * units, units)], target, sems.at[3 * n + 2]))
    for k in range(2):
        for copy in first[k * len(weights) : (k + 1) * len(weights)]:
            copy.start()
        for copy in last[k * len(weights) // 2 : (k + 1) * len(weights) // 2]:
            copy.start()
    count = part.shape[0]
    per = count // rows
    inputs = part[...]
    result = None
    chunk = total // 2
    for k in range(2):
        lo = k * chunk
        for copy in first[k * len(weights) : (k + 1) * len(weights)]:
            copy.wait()
        gate, up = [
            lax.dot_general(
                inputs, held[at : at + chunk], (((1,), (1,)), ((), ())), preferred_element_type=F32
            )
            for at in (lo, total + lo)
        ]
        hidden = (gate / (1.0 + jnp.exp(-gate)) * up).astype(BF16)
        for copy in last[k * len(weights) // 2 : (k + 1) * len(weights) // 2]:
            copy.wait()
        term = dot(hidden, held_down[lo : lo + chunk])
        result = term if result is None else result + term
    width = result.shape[1] // SUB
    for j in range(SUB):
        tiles[:, j, :] = result[:, j * width : (j + 1) * width]
    z = lax.axis_index("z")
    for i in range(rows):
        tiles[z * rows + i] = tiles[z * rows + i] + mixed[i]
    for i in range(rows):
        for n in range(per):
            out[i * per + n] = tiles[n * rows + i].astype(BF16)


def call(kernel, out_shape, args, smem=0, hbm=(), out_specs=None, scratch=(), limit=12 << 20, cost=None):
    vmem = pl.BlockSpec(memory_space=pltpu.VMEM)
    scalar = pl.BlockSpec(memory_space=pltpu.SMEM)
    specs = [scalar] * smem + [vmem] * (len(args) - smem)
    args = list(args)
    for i in hbm:
        specs[i] = pl.BlockSpec(memory_space=pltpu.HBM)
        args[i] = pltpu.with_memory_space_constraint(args[i], pltpu.HBM)
    return pl.pallas_call(
        kernel,
        out_shape=out_shape,
        in_specs=specs,
        out_specs=jax.tree.map(lambda _: vmem, out_shape) if out_specs is None else out_specs,
        scratch_shapes=scratch,
        compiler_params=pltpu.CompilerParams(vmem_limit_bytes=limit),
        cost_estimate=cost,
    )(*args)


def body(
    tokens, attn_gain, w_qkv, w_out, mlp_gain, w_gate_up, w_down, kv_cache, block_owner, block_fill
):
    groups = lax.axis_size("grp")
    z_chips = lax.axis_size("z")
    x_chips = lax.axis_size("x")
    chips = z_chips * x_chips
    rows, features = tokens.shape
    head_dim = features // HEADS
    blocks = kv_cache.shape[0]
    units = w_down.shape[0]
    half = rows * chips
    count = blocks + rows
    width = features // SUB
    swap = [(0, 1), (1, 0)]
    every = ("grp",) + CHIP
    sizes = dict(rows=rows, chips=chips)

    def shape(kind, *dims):
        return jax.ShapeDtypeStruct(dims, kind)

    def tiles(n):
        return pltpu.VMEM((n, SUB, width), F32)

    sent, packed = call(
        lambda *refs: spread_kernel(*refs, chips=chips),
        (shape(BF16, groups * chips, SUB, width), shape(BF16, 3 * units, features)),
        (tokens, jnp.swapaxes(w_gate_up, 1, 2), w_down),
        hbm=(0, 1, 2),
        scratch=[pltpu.VMEM((rows, features), BF16), tiles(rows), pltpu.SemaphoreType.DMA((4,))],
        cost=pl.CostEstimate(flops=10**11, transcendentals=0, bytes_accessed=1 << 18),
    )
    weights = [packed] + [
        lax.ppermute(packed, "x", [(i, (i + k) % x_chips) for i in range(x_chips)])
        for k in range(1, x_chips)
    ]
    got = lax.all_to_all(sent, every, 0, 0, tiled=True)
    peer = lax.ppermute(got, "core", swap)
    weights = weights + [lax.ppermute(weight, "core", swap) for weight in weights]
    gain = attn_gain.reshape(1, features)
    partial = call(
        lambda *refs: attend_kernel(*refs, head_dim=head_dim, **sizes),
        shape(F32, count, features + 2 * LANES),
        (block_owner, block_fill, got, peer, gain, w_qkv, kv_cache),
        smem=2,
        scratch=[tiles(blocks)],
    )
    got, partial = lax.optimization_barrier((got, partial))
    partial_peer = lax.ppermute(partial, "core", swap)
    own, inputs = call(
        lambda *refs: own_kernel(*refs, head_dim=head_dim, **sizes),
        (shape(F32, SUB, features + 2 * LANES), shape(F32, SUB, features)),
        (got, gain, w_qkv),
        scratch=[tiles(SUB)],
        cost=pl.CostEstimate(flops=1, transcendentals=0, bytes_accessed=1),
    )
    sent = call(
        lambda *refs: merge_kernel(*refs, rows=rows, head_dim=head_dim),
        shape(BF16, chips, rows, features + LANES),
        (partial, own, partial_peer),
        scratch=[
            pltpu.VMEM((half, features + LANES), F32),
            pltpu.VMEM((count, features + 2 * LANES), F32),
        ],
    )
    got = lax.all_to_all(sent, CHIP, 0, 0, tiled=True)
    mixed, sent = call(
        lambda *refs: project_kernel(*refs, rows=rows, head_dim=head_dim),
        (shape(F32, SUB, SUB, width), shape(BF16, rows * z_chips, features)),
        (got, inputs, w_out, mlp_gain.reshape(1, features)),
        scratch=[pltpu.VMEM((half, features + LANES), F32)],
    )
    got = lax.all_to_all(sent, "z", 0, 0, tiled=True)
    sent = call(
        lambda *refs: hidden_kernel(*refs, rows=rows),
        shape(BF16, rows * z_chips, SUB, width),
        [got, mixed] + weights,
        hbm=range(2, 2 + len(weights)),
        scratch=[
            pltpu.VMEM((2 * len(weights) * units, features), BF16),
            pltpu.VMEM((len(weights) * units, features), BF16),
            tiles(rows * z_chips),
            pltpu.SemaphoreType.DMA((3 * len(weights),)),
        ],
    )
    got = lax.all_to_all(sent, ("grp", "z"), 0, 0, tiled=True)
    return call(
        finish_kernel,
        shape(BF16, rows, features),
        (got,),
        scratch=[tiles(rows)],
    )


def solution(mesh):
    groups, shards = mesh.devices.shape
    devices = mesh.devices.reshape(groups, -1, X_CHIPS, CORES)
    fine = Mesh(devices, ("grp",) + CHIP + ("core",))
    seq = CHIP + ("core",)
    whole = ("grp",) + seq
    in_specs = (
        P(whole, None),
        P(),
        P(),
        P(),
        P(),
        P(None, None, seq),
        P(seq, None),
        P(whole, None, None, None),
        P(whole),
        P(whole),
    )
    return jax.shard_map(
        body, mesh=fine, in_specs=in_specs, out_specs=P(whole, None), check_vma=False
    )
```
